512 devices in a mesh: dp: 64 (over z_lo, y, core), tile: 8 (over x, z_hi).
Axes of the slice: x: 4, y: 4, z: 16 (z_hi: 2, z_lo: 8; z = z_hi * 8 + z_lo), core: 2. Of those that a mesh axis runs over, the one named last changes fastest.
Arguments:
- frames: bfloat16 [64, 2, 3, 128, 128], P('dp', None, None, 'tile'), may hold values from 0 to 1
- features: bfloat16 [64, 64, 128, 128], P('dp', None, 'tile'), may hold values from -16 to 16
- cotangent: float32 [64, 3, 128, 128], P('dp', None, 'tile'), may hold values from -6 to 6
- head_weight: bfloat16 [108, 576], replicated, may hold values from -0.25 to 0.25
Outputs:
- grad_weight: float32 [108, 576], replicated
- grad_features: float32 [64, 64, 128, 128], P('dp', None, 'tile')
- grad_frames: float32 [64, 2, 3, 128, 128], P('dp', None, None, 'tile')
The draws below stay inside these ranges and needn't reach their ends.
All inputs are finite; a program needn't handle non-finite values.
Results may differ from the reference program's by a relative error of at most 0.003.
Values may be sent and summed in bfloat16 or wider, within the bound.
No kernel may reach another device: no remote copies, remote signals or barrier semaphores. Data moves between devices by JAX's collectives and lax.ppermute only.
A program may use at most 64 MiB of HBM per device.

```python
import jax
import jax.numpy as jnp
from jax import lax

C = 64
W = 128
KOUT = 108
H = 128
PAIRS = 64


def spiked(entries, own_key, source, target, blocks, factor):
    def block_of(dim):
        return (jnp.arange(entries.shape[dim]) // (entries.shape[dim] // blocks)).reshape((-1,) + (1,) * (entries.ndim - 1 - dim))

    near = jax.random.permutation(own_key, blocks)[block_of(target)]
    second = (block_of(target) + blocks // 2) % blocks
    return jnp.where((block_of(source) == near) | (block_of(source) == second), factor * entries, entries)


def shard_levels(rng, extent, pieces, smallest, largest):
    factor_of, own = 1.0, jax.random.fold_in(rng, 6)
    for dim, shards_of in pieces:
        heights = jnp.exp(jax.random.uniform(jax.random.fold_in(own, dim), (shards_of,), jnp.float32, smallest / len(pieces), largest / len(pieces)))
        factor_of = factor_of * jnp.repeat(heights, extent[dim] // shards_of).reshape([-1 if axis == dim else 1 for axis in range(len(extent))])
    return factor_of


def normal_values(rng, dims, scale, limit, split=(), held_as=jnp.bfloat16):
    loudness = shard_levels(rng, dims, split, -0.22, 0.18) if split else 1.0
    result = jax.random.normal(rng, dims, jnp.float32) * scale * loudness
    return jnp.minimum(jnp.maximum(result, -limit), limit).astype(held_as)


def noise_with(key, dims, deviation, limit, shards, heavy, kind=jnp.bfloat16):
    result = deviation * jax.random.normal(key, dims, jnp.float32)
    if shards:
        result = result * shard_levels(key, dims, shards, -0.22, 0.18)
    return jnp.clip(spiked(result, jax.random.fold_in(key, 3), *heavy), -limit, limit).astype(kind)


def setup_inputs(seed: int = 0) -> dict:
    key_list = jax.random.split(jax.random.key(seed), 5)
    return {
        "frames": jnp.clip(1.0 * jax.random.uniform(key_list[0], (PAIRS, 2, 3, H, W), jnp.float32) ** shard_levels(key_list[0], (PAIRS, 2, 3, H, W), ((0, 64), (3, 8)), -0.2, 0.2), 0.0, 1.0).astype(jnp.bfloat16),
        "features": noise_with(key_list[1], (PAIRS, C, H, W), 1.0, 16.0, ((0, 64), (2, 8)), (0, 1, 64, 4.0)),
        "cotangent": normal_values(key_list[2], (PAIRS, 3, H, W), 1.0, 6.0, ((0, 64), (2, 8)), jnp.float32),
        "head_weight": normal_values(key_list[3], (KOUT, 9 * C), (9 * C) ** -0.5, 0.25),
    }


def make_patches(padded_map, row_count, col_count):
    blocks = []
    for row_shift in range(3):
        for col_shift in range(3):
            piece = padded_map[:, row_shift:row_shift + row_count, col_shift:col_shift + col_count]
            blocks.append(piece.reshape(piece.shape[0], row_count * col_count))
    return jnp.concatenate(blocks, 0)


def fold_patches(patch_grad, channels, row_count, col_count):
    folded = jnp.zeros((channels, row_count + 2, col_count + 2), jnp.float32)
    slot_index = 0
    for row_shift in range(3):
        for col_shift in range(3):
            block = patch_grad[slot_index * channels:(slot_index + 1) * channels].reshape(channels, row_count, col_count)
            folded = folded.at[:, row_shift:row_shift + row_count, col_shift:col_shift + col_count].add(block)
            slot_index += 1
    return folded


def separable_grads(padded, vertical, horizontal, upstream, group_size):
    tap_count = vertical.shape[0]
    row_count = upstream.shape[1]
    col_count = upstream.shape[2]
    highest = lax.Precision.HIGHEST

    def one_tap(tap_index, carried):
        grad_vert, grad_horiz, grad_padded = carried
        tap_band = lax.dynamic_slice_in_dim(padded, tap_index, row_count, 1)
        window = jnp.stack([tap_band[:, :, col_tap:col_tap + col_count] for col_tap in range(tap_count)])
        blended = jnp.einsum('jyx,jcyx->cyx', horizontal, window, precision=highest)
        grad_vert = lax.dynamic_update_slice_in_dim(grad_vert, jnp.sum(upstream * blended, 0)[None], tap_index, 0)
        scaled = lax.dynamic_index_in_dim(vertical, tap_index, 0, keepdims=False)[None] * upstream
        grad_horiz = grad_horiz + jnp.einsum('cyx,jcyx->jyx', scaled, window, precision=highest)
        spread = horizontal[:, None] * scaled[None]
        back_sum = jnp.zeros((3, row_count, col_count + tap_count - 1), jnp.float32)
        for col_tap in range(tap_count):
            back_sum = back_sum.at[:, :, col_tap:col_tap + col_count].add(spread[col_tap])
        old_rows = lax.dynamic_slice_in_dim(grad_padded, tap_index, row_count, 1)
        grad_padded = lax.dynamic_update_slice_in_dim(grad_padded, old_rows + back_sum, tap_index, 1)
        return grad_vert, grad_horiz, grad_padded

    def group_step(group_index, carried):
        for offset in range(group_size):
            carried = one_tap(group_index * group_size + offset, carried)
        return carried

    start_state = (jnp.zeros(vertical.shape, jnp.float32), jnp.zeros(vertical.shape, jnp.float32),
                   jnp.zeros(padded.shape, jnp.float32))
    return lax.fori_loop(0, tap_count // group_size, group_step, start_state)


def reference(frames, features, cotangent, head_weight):
    tap_count = head_weight.shape[0] // 4
    rim_rows = (tap_count - 1) // 2
    kernel_scale = tap_count ** -0.5

    def one_pair(pair_items):
        pair_frames, feature_map, upstream = pair_items
        channels, row_count, col_count = feature_map.shape
        patches = make_patches(jnp.pad(feature_map, ((0, 0), (1, 1), (1, 1))), row_count, col_count)
        kernels = jnp.dot(head_weight, patches, preferred_element_type=jnp.float32).reshape(-1, row_count, col_count)
        grad_list = []
        frame_list = []
        for which_frame in range(2):
            vertical = kernels[2 * which_frame * tap_count:(2 * which_frame + 1) * tap_count] * kernel_scale
            horizontal = kernels[(2 * which_frame + 1) * tap_count:(2 * which_frame + 2) * tap_count] * kernel_scale
            padded = jnp.pad(pair_frames[which_frame].astype(jnp.float32), ((0, 0), (rim_rows, rim_rows), (rim_rows, rim_rows)))
            grad_vert, grad_horiz, grad_padded = separable_grads(padded, vertical, horizontal, upstream, 1)
            grad_list += [grad_vert, grad_horiz]
            frame_list.append(grad_padded[:, rim_rows:rim_rows + row_count, rim_rows:rim_rows + col_count])
        kernel_grad = (jnp.concatenate(grad_list, 0) * kernel_scale).astype(jnp.bfloat16)
        flat_grad = kernel_grad.reshape(kernel_grad.shape[0], row_count * col_count)
        weight_part = lax.dot_general(flat_grad, patches, (((1,), (1,)), ((), ())), preferred_element_type=jnp.float32)
        patch_grad = lax.dot_general(head_weight, flat_grad, (((0,), (0,)), ((), ())), preferred_element_type=jnp.float32)
        feat_grad = fold_patches(patch_grad, channels, row_count, col_count)[:, 1:row_count + 1, 1:col_count + 1]
        return weight_part, feat_grad, jnp.stack(frame_list)

    pair_parts, feat_grads, frame_grads = lax.map(one_pair, (frames, features, cotangent))
    pixel_count = frames.shape[0] * frames.shape[3] * frames.shape[4]
    weight_sum = jnp.sum(pair_parts, 0) * (pixel_count ** -0.5)
    return weight_sum, feat_grads, frame_grads
```

```python
import functools
import jax
import jax.numpy as jnp
from jax import lax
from jax.experimental import pallas as pl
from jax.experimental.pallas import tpu as pltpu
from jax.sharding import Mesh, PartitionSpec as P

F32, BF16 = jnp.float32, jnp.bfloat16
UNROLL = 4


def dims(a, b):
    return (((a,), (b,)), ((), ()))


def split(v):
    hi = v.astype(BF16)
    lo = (v - hi.astype(F32)).astype(BF16)
    return hi, lo


def row_kernel(taps, feat, halo_up, halo_dn, frames, cot, wfwd, wbwd,
               parts_ref, gfeat, gframe, rim_up, rim_dn,
               fs, fb, ip, gf, acc, wg, flat):
    rim = (taps - 1) // 2
    channels, rows, width = feat.shape
    scale = taps ** -0.5
    lane = lax.broadcasted_iota(jnp.int32, (width, width), 1)
    sub = lax.broadcasted_iota(jnp.int32, (width, width), 0)
    first, last = lane[:channels] == 0, lane[:channels] == width - 1

    fs[...] = feat[...].astype(F32).reshape(channels * rows, width)

    def put(at, row):
        left = jnp.where(first, 0.0, pltpu.roll(row, 1, 1))
        right = jnp.where(last, 0.0, pltpu.roll(row, width - 1, 1))
        fb[at] = jnp.concatenate([left, row, right], 0).astype(BF16)

    put(0, halo_up[:channels].astype(F32))
    put(rows + 1, halo_dn[:channels].astype(F32))
    for y in range(rows):
        put(y + 1, fs[pl.ds(y, channels, stride=rows), :])

    for n in range(6):
        f, c = divmod(n, 3)
        at = channels + n * rim
        turn = rim + 64 * f
        ip[n] = jnp.zeros(ip.shape[1:], F32)
        ip[n, :rim] = halo_up[at:at + rim].astype(F32)
        ip[n, rim:rim + rows] = frames[f, c].astype(F32)
        ip[n, rim + rows:rim + rows + rim] = halo_dn[at:at + rim].astype(F32)
        ip[n] = pltpu.roll(ip[n], turn, 1)
    gf[...] = jnp.zeros_like(gf)
    acc[...] = jnp.zeros_like(acc)
    wg[...] = jnp.zeros_like(wg)

    bands = []
    for f in range(2):
        tap = (lane - sub + (2 * width - 64 * f)) % width
        at = sub + tap - rim
        bands.append((tap < taps) & (at >= 0) & (at < width))

    def step(y, carry):
        patches = fb[pl.ds(y, 3)].reshape(9 * channels, width)
        k = jnp.dot(wfwd[...], patches, preferred_element_type=F32) * scale
        skew = pltpu.roll(k.T, 0, 1, stride=1, stride_axis=0)
        g = [cot[c, pl.ds(y, 1), :] for c in range(3)]
        grads = []
        horiz = None
        for f in range(2):
            v = k[64 * f + 32:64 * f + 64]
            u = jnp.concatenate([v * g[c] for c in range(3)], 0)
            window = jnp.concatenate(
                [ip[3 * f + c, pl.ds(y, 32), :] for c in range(3)], 0).astype(BF16)
            b = jnp.where(bands[f], skew, 0.0)
            b_hi, b_lo = split(b)
            u_hi, u_lo = split(u)
            blended = lax.dot_general(
                jnp.concatenate([window, window], 1), jnp.concatenate([b_hi, b_lo], 1),
                dims(1, 1), preferred_element_type=F32)
            grads.append(sum(g[c] * blended[32 * c:32 * c + 32] for c in range(3)))
            d = lax.dot_general(
                jnp.concatenate([u_hi, u_lo], 0), jnp.concatenate([window, window], 0),
                dims(0, 0), preferred_element_type=F32)
            horiz = jnp.where(bands[0], d, 0.0) if f == 0 else jnp.where(bands[1], d, horiz)
            w = jnp.dot(
                jnp.concatenate([u_hi, u_hi, u_lo], 1),
                jnp.concatenate([b_hi, b_lo, b_hi], 0), preferred_element_type=F32)
            for c in range(3):
                gf[3 * f + c, pl.ds(y, 32), :] += w[32 * c:32 * c + 32]
        parts = []
        for r in range(width // 8):
            p = horiz[8 * r:8 * r + 8]
            if r:
                p = pltpu.roll(p, width - 8 * r, 1)
            parts.append(p)
        horiz = jnp.concatenate(parts, 0)
        for bit in range(3):
            horiz = jnp.where((sub & (1 << bit)) != 0, pltpu.roll(horiz, width - (1 << bit), 1), horiz)
        ht = horiz.T
        kg = jnp.concatenate([ht[:32], grads[0], ht[64:96], grads[1]], 0) * scale
        kgb = kg.astype(BF16)
        wg[...] += lax.dot_general(kgb, patches, dims(1, 1), preferred_element_type=F32)
        kgr = kgb.astype(F32)
        wide = jnp.concatenate([
            jnp.where(lane == width - 1, 0.0, pltpu.roll(kgr, width - 1, 1)),
            kgr,
            jnp.where(lane == 0, 0.0, pltpu.roll(kgr, 1, 1))], 0).astype(BF16)
        part = jnp.dot(wbwd[...], wide, preferred_element_type=F32)
        for a in range(3):
            acc[y + a] += part[channels * a:channels * (a + 1)]
        return carry

    lax.fori_loop(0, rows, step, 0, unroll=UNROLL)

    for y in range(rows):
        gfeat[pl.ds(y, channels, stride=rows), :] = acc[y + 1]
    rim_up[:channels] = acc[0].astype(BF16)
    rim_dn[:channels] = acc[rows + 1].astype(BF16)
    for n in range(6):
        gf[n] = pltpu.roll(gf[n], width - rim - 64 * (n // 3), 1)
        gframe[n] = gf[n, rim:rim + rows]
        at = channels + n * rim
        rim_up[at:at + rim] = gf[n, :rim].astype(BF16)
        rim_dn[at:at + rim] = gf[n, rim + rows:rim + rows + rim].astype(BF16)
    pack(wg[...], flat)
    count, size = parts_ref.shape[:2]
    for n in range(count):
        parts_ref[n] = flat[size * n:size * (n + 1)]


def pack(value, flat):
    full = value.shape[1] // 128
    for n in range(full):
        flat[128 * n:128 * (n + 1)] = value[:, 128 * n:128 * (n + 1)]
    tail = value[:, 128 * full:]
    flat[128 * full:] = jnp.concatenate([tail[:64], tail[64:]], 1)


def unpack_kernel(taps, factor, parts_ref, out, flat):
    count, size = parts_ref.shape[:2]
    for n in range(count):
        flat[size * n:size * (n + 1)] = parts_ref[n]
    full = out.shape[1] // 128
    tail = flat[128 * full:]
    blocks = [flat[128 * n:128 * (n + 1)] for n in range(full)]
    blocks.append(jnp.concatenate([tail[:, :64], tail[:, 64:]], 0))
    value = jnp.concatenate(blocks, 1) * factor
    for n, group in enumerate((1, 0, 3, 2)):
        out[taps * n:taps * (n + 1)] = value[32 * group:32 * group + taps]


def order(hw, taps):
    hw = hw.reshape(2, 2, taps, -1)[:, ::-1]
    return jnp.pad(hw, ((0, 0), (0, 0), (0, 32 - taps), (0, 0))).reshape(128, -1)


def local_grads(feat, halo_up, halo_dn, frames, cot, hw, parts):
    channels, rows, width = feat.shape
    taps = hw.shape[0] // 4
    rim = (taps - 1) // 2
    columns = 9 * channels
    wfwd = order(hw, taps)
    wbwd = wfwd.reshape(128, 3, 3, channels).transpose(1, 3, 2, 0).reshape(3 * channels, 3 * 128)
    vm = pl.BlockSpec(memory_space=pltpu.VMEM)
    return pl.pallas_call(
        functools.partial(row_kernel, taps),
        out_shape=(
            jax.ShapeDtypeStruct((parts, columns // parts, 128), F32),
            jax.ShapeDtypeStruct((channels * rows, width), F32),
            jax.ShapeDtypeStruct((6, rows, width), F32),
            jax.ShapeDtypeStruct((channels + 6 * rim, width), BF16),
            jax.ShapeDtypeStruct((channels + 6 * rim, width), BF16),
        ),
        in_specs=[vm] * 7,
        out_specs=[vm] * 5,
        scratch_shapes=[
            pltpu.VMEM((channels * rows, width), F32),
            pltpu.VMEM((rows + 2, 3 * channels, width), BF16),
            pltpu.VMEM((6, rows + 32, width), F32),
            pltpu.VMEM((6, rows + 32, width), F32),
            pltpu.VMEM((rows + 2, channels, width), F32),
            pltpu.VMEM((128, columns), F32),
            pltpu.VMEM((columns, 128), F32),
        ],
    )(feat, halo_up, halo_dn, frames, cot, wfwd, wbwd)


def unpack(parts, taps, factor):
    count, size, _ = parts.shape
    vm = pl.BlockSpec(memory_space=pltpu.VMEM)
    return pl.pallas_call(
        functools.partial(unpack_kernel, taps, factor),
        out_shape=jax.ShapeDtypeStruct((4 * taps, count * size), F32),
        in_specs=[vm],
        out_specs=vm,
        scratch_shapes=[pltpu.VMEM((count * size, 128), F32)],
    )(parts)


PLANE, LINE, TILE = ("y", "core", "x"), ("zl", "zh"), ("x", "zh")


def spread(value, axes, count):
    return lax.all_to_all(jnp.broadcast_to(value[None], (count,) + value.shape), axes, 0, 0)


def shards(frames, features, cotangent, head_weight):
    taps = head_weight.shape[0] // 4
    rim = (taps - 1) // 2
    feat, frame, cot = features[0], frames[0], cotangent[0]
    channels, rows, width = feat.shape
    tiles, plane, line = lax.axis_size(TILE), lax.axis_size(PLANE), lax.axis_size(LINE)
    down = [(i, i + 1) for i in range(tiles - 1)]
    up = [(i + 1, i) for i in range(tiles - 1)]

    def halo(row, part):
        return jnp.concatenate([feat[:, row], part.reshape(6 * rim, width)], 0)

    halo_up = lax.ppermute(halo(rows - 1, frame[:, :, rows - rim:]), TILE, down)
    halo_dn = lax.ppermute(halo(0, frame[:, :, :rim]), TILE, up)
    parts, gfeat, gframe, rim_up, rim_dn = local_grads(
        feat, halo_up, halo_dn, frame, cot, head_weight, plane)

    from_up = lax.ppermute(rim_dn, TILE, down).astype(F32)
    from_dn = lax.ppermute(rim_up, TILE, up).astype(F32)

    own = jnp.sum(lax.all_to_all(parts, PLANE, 0, 0), 0)
    own = jnp.sum(spread(own, LINE, line), 0)
    total = spread(own, PLANE, plane)
    pixels = plane * line * rows * width
    grad_weight = unpack(total, taps, pixels ** -0.5)

    gfeat = gfeat.reshape(channels, rows, width)
    gfeat = (gfeat + jnp.pad(from_up[:channels, None], ((0, 0), (0, rows - 1), (0, 0)))
             + jnp.pad(from_dn[:channels, None], ((0, 0), (rows - 1, 0), (0, 0))))
    gframe = (gframe
              + jnp.pad(from_up[channels:].reshape(6, rim, width), ((0, 0), (0, rows - rim), (0, 0)))
              + jnp.pad(from_dn[channels:].reshape(6, rim, width), ((0, 0), (rows - rim, 0), (0, 0))))
    return grad_weight, gfeat[None], gframe.reshape(1, 2, 3, rows, width)


def solution(mesh):
    fine = Mesh(mesh.devices.reshape(8, 4, 2, 4, 2), ("zl", "y", "core", "x", "zh"))
    pairs, tile = ("zl", "y", "core"), ("x", "zh")
    in_specs = (
        P(pairs, None, None, tile, None),
        P(pairs, None, tile, None),
        P(pairs, None, tile, None),
        P(),
    )
    out_specs = (P(), P(pairs, None, tile, None), P(pairs, None, None, tile, None))
    return jax.shard_map(shards, mesh=fine, in_specs=in_specs, out_specs=out_specs, check_vma=False)
```

```python
import functools
import jax
import jax.numpy as jnp
from jax import lax
from jax.experimental import pallas as pl
from jax.experimental.pallas import tpu as pltpu
from jax.sharding import Mesh, PartitionSpec as P


F32, BF16 = jnp.float32, jnp.bfloat16
UNROLL_EARLY = 7
UNROLL_LATE = 7
VMEM_GRANT = 16 * 1024 * 1024


def dims(a, b):
    return (((a,), (b,)), ((), ()))


def split(v):
    hi = v.astype(BF16)
    lo = (v - hi.astype(F32)).astype(BF16)
    return hi, lo


def column_bands(taps, width):
    rim = (taps - 1) // 2
    lane = lax.broadcasted_iota(jnp.int32, (width, width), 1)
    sub = lax.broadcasted_iota(jnp.int32, (width, width), 0)
    bands = []
    for f in range(2):
        tap = (lane - sub + (2 * width - 64 * f)) % width
        at = sub + tap - rim
        bands.append((tap < taps) & (at >= 0) & (at < width))
    return lane, sub, bands


def three_columns(row):
    lane = lax.broadcasted_iota(jnp.int32, row.shape, 1)
    width = row.shape[1]
    left = jnp.where(lane == 0, 0.0, pltpu.roll(row, 1, 1))
    right = jnp.where(lane == width - 1, 0.0, pltpu.roll(row, width - 1, 1))
    return jnp.concatenate([left, row, right], 0).astype(BF16)


def frame_terms(taps, k, g, bands):
    skew = pltpu.roll((k * taps ** -0.5).T, 0, 1, stride=1, stride_axis=0)
    out = []
    for f in range(2):
        v = k[64 * f + 32:64 * f + 64] * taps ** -0.5
        u_hi, u_lo = split(jnp.concatenate([v * g[c] for c in range(3)], 0))
        b_hi, b_lo = split(jnp.where(bands[f], skew, 0.0))
        w = jnp.dot(
            jnp.concatenate([u_hi, u_hi, u_lo], 1),
            jnp.concatenate([b_hi, b_lo, b_hi], 0), preferred_element_type=F32)
        out.append((jnp.concatenate([b_hi, b_lo], 1), jnp.concatenate([u_hi, u_lo], 0), w))
    return out


def early_kernel(taps, feat, cot, wfwd, fb, bst, ust, gf, fs):
    channels, rows, width = feat.shape
    fs[...] = feat[...].astype(F32).reshape(channels * rows, width)
    for y in range(rows):
        fb[y] = three_columns(fs[pl.ds(y, channels, stride=rows), :])
    gf[...] = jnp.zeros_like(gf)
    _, _, bands = column_bands(taps, width)

    def step(m, carry):
        ya = 2 * m + 1
        pair = jnp.concatenate(
            [fb[pl.ds(ya + h - 1, 3)].reshape(9 * channels, width) for h in range(2)], 1)
        k = jnp.dot(wfwd[...], pair, preferred_element_type=F32)
        for h in range(2):
            y = ya + h
            g = [cot[c, pl.ds(y, 1), :] for c in range(3)]
            terms = frame_terms(taps, k[:, width * h:width * (h + 1)], g, bands)
            for f, (b, u, w) in enumerate(terms):
                bst[y - 1, f] = b
                ust[y - 1, f] = u
                for c in range(3):
                    gf[3 * f + c, pl.ds(y, 32), :] += w[32 * c:32 * c + 32]
        return carry

    lax.fori_loop(0, rows // 2 - 1, step, 0, unroll=UNROLL_EARLY)


def late_kernel(taps, halo_up, halo_dn, frames, cot, wfwd, wbwd, fb, bst, ust, gf_in,
                parts_ref, gfeat, gframe, rim_up, rim_dn,
                ip, gf, acc, wg, flat):
    rim = (taps - 1) // 2
    rows, channels, width = fb.shape[0], fb.shape[1] // 3, fb.shape[2]
    lane, sub, bands = column_bands(taps, width)
    head = three_columns(halo_up[:channels].astype(F32))
    foot = three_columns(halo_dn[:channels].astype(F32))
    edges = jnp.concatenate([
        jnp.concatenate([head, fb[0], fb[1]], 0),
        jnp.concatenate([fb[rows - 2], fb[rows - 1], foot], 0)], 1)
    k = jnp.dot(wfwd[...], edges, preferred_element_type=F32)

    for n in range(6):
        f, c = divmod(n, 3)
        at = channels + n * rim
        ip[n] = jnp.zeros(ip.shape[1:], F32)
        ip[n, :rim] = halo_up[at:at + rim].astype(F32)
        ip[n, rim:rim + rows] = frames[f, c].astype(F32)
        ip[n, rim + rows:rim + rows + rim] = halo_dn[at:at + rim].astype(F32)
        ip[n] = pltpu.roll(ip[n], rim + 64 * f, 1)
    gf[...] = gf_in[...]
    acc[...] = jnp.zeros_like(acc)
    wg[...] = jnp.zeros_like(wg)

    def tap_grads(y, terms):
        g = [cot[c, pl.ds(y, 1), :] for c in range(3)]
        grads = []
        horiz = None
        for f, (b, u) in enumerate(terms):
            window = jnp.concatenate(
                [ip[3 * f + c, pl.ds(y, 32), :] for c in range(3)], 0).astype(BF16)
            blended = lax.dot_general(
                jnp.concatenate([window, window], 1), b, dims(1, 1), preferred_element_type=F32)
            grads.append(sum(g[c] * blended[32 * c:32 * c + 32] for c in range(3)))
            d = lax.dot_general(
                u, jnp.concatenate([window, window], 0), dims(0, 0), preferred_element_type=F32)
            horiz = jnp.where(bands[f], d, 0.0 if f == 0 else horiz)
        turned = [horiz[:8]]
        for r in range(1, width // 8):
            turned.append(pltpu.roll(horiz[8 * r:8 * r + 8], width - 8 * r, 1))
        horiz = jnp.concatenate(turned, 0)
        for bit in range(3):
            horiz = jnp.where((sub & (1 << bit)) != 0, pltpu.roll(horiz, width - (1 << bit), 1), horiz)
        ht = horiz.T
        kg = jnp.concatenate([ht[:32], grads[0], ht[64:96], grads[1]], 0) * taps ** -0.5
        return kg.astype(BF16)

    def accumulate(ya, yb, pair, kga, kgb):
        wg[...] += lax.dot_general(
            jnp.concatenate([kga, kgb], 1), pair, dims(1, 1), preferred_element_type=F32)
        wide = []
        for kg in (kga, kgb):
            kgr = kg.astype(F32)
            wide.append(jnp.concatenate([
                jnp.where(lane == width - 1, 0.0, pltpu.roll(kgr, width - 1, 1)),
                kgr,
                jnp.where(lane == 0, 0.0, pltpu.roll(kgr, 1, 1))], 0).astype(BF16))
        part = jnp.dot(wbwd[...], jnp.concatenate(wide, 1), preferred_element_type=F32)
        for a in range(3):
            acc[ya + a] += part[channels * a:channels * (a + 1), :width]
            acc[yb + a] += part[channels * a:channels * (a + 1), width:]

    kgs = []
    for h, y in enumerate((0, rows - 1)):
        g = [cot[c, y:y + 1, :] for c in range(3)]
        terms = frame_terms(taps, k[:, width * h:width * (h + 1)], g, bands)
        for f, (_, _, w) in enumerate(terms):
            for c in range(3):
                gf[3 * f + c, y:y + 32] += w[32 * c:32 * c + 32]
        kgs.append(tap_grads(y, [t[:2] for t in terms]))
    accumulate(0, rows - 1, edges, *kgs)

    def step(m, carry):
        ya = 2 * m + 1
        pair = jnp.concatenate(
            [fb[pl.ds(ya + h - 1, 3)].reshape(9 * channels, width) for h in range(2)], 1)
        kga, kgb = [
            tap_grads(ya + h, [(bst[ya + h - 1, f], ust[ya + h - 1, f]) for f in range(2)])
            for h in range(2)]
        accumulate(ya, ya + 1, pair, kga, kgb)
        return carry

    lax.fori_loop(0, rows // 2 - 1, step, 0, unroll=UNROLL_LATE)

    for y in range(rows):
        gfeat[pl.ds(y, channels, stride=rows), :] = acc[y + 1]
    rim_up[:channels] = acc[0].astype(BF16)
    rim_dn[:channels] = acc[rows + 1].astype(BF16)
    for n in range(6):
        gf[n] = pltpu.roll(gf[n], width - rim - 64 * (n // 3), 1)
        gframe[n] = gf[n, rim:rim + rows]
        at = channels + n * rim
        rim_up[at:at + rim] = gf[n, :rim].astype(BF16)
        rim_dn[at:at + rim] = gf[n, rim + rows:rim + rows + rim].astype(BF16)
    pack(wg[...], flat)
    count, size = parts_ref.shape[:2]
    for n in range(count):
        parts_ref[n] = flat[size * n:size * (n + 1)]


def pack(value, flat):
    full = value.shape[1] // 128
    for n in range(full):
        flat[128 * n:128 * (n + 1)] = value[:, 128 * n:128 * (n + 1)]
    tail = value[:, 128 * full:]
    flat[128 * full:] = jnp.concatenate([tail[:64], tail[64:]], 1)


def unpack_kernel(taps, factor, parts_ref, out, flat):
    count, size = parts_ref.shape[:2]
    for n in range(count):
        flat[size * n:size * (n + 1)] = parts_ref[n].astype(F32)
    full = out.shape[1] // 128
    tail = flat[128 * full:]
    blocks = [flat[128 * n:128 * (n + 1)] for n in range(full)]
    blocks.append(jnp.concatenate([tail[:, :64], tail[:, 64:]], 0))
    value = jnp.concatenate(blocks, 1) * factor
    for n, group in enumerate((1, 0, 3, 2)):
        out[taps * n:taps * (n + 1)] = value[32 * group:32 * group + taps]


def order(hw, taps):
    hw = hw.reshape(2, 2, taps, -1)[:, ::-1]
    return jnp.pad(hw, ((0, 0), (0, 0), (0, 32 - taps), (0, 0))).reshape(128, -1)


def vmem_call(kernel, outs, scratch, *operands):
    vm = pl.BlockSpec(memory_space=pltpu.VMEM)
    return pl.pallas_call(
        kernel,
        out_shape=[jax.ShapeDtypeStruct(*o) for o in outs],
        in_specs=[vm] * len(operands),
        out_specs=[vm] * len(outs),
        scratch_shapes=[pltpu.VMEM(*o) for o in scratch],
        compiler_params=pltpu.CompilerParams(vmem_limit_bytes=VMEM_GRANT),
    )(*operands)


def early(feat, cot, wfwd, taps):
    channels, rows, width = feat.shape
    return vmem_call(
        functools.partial(early_kernel, taps),
        [((rows, 3 * channels, width), BF16), ((rows - 2, 2, width, 2 * width), BF16),
         ((rows - 2, 2, 192, width), BF16), ((6, rows + 32, width), F32)],
        [((channels * rows, width), F32)],
        feat, cot, wfwd)


def late(halo_up, halo_dn, frames, cot, wfwd, wbwd, held, taps, parts):
    rows, width = held[0].shape[0], held[0].shape[2]
    channels = held[0].shape[1] // 3
    columns = 9 * channels
    rim_shape = (halo_up.shape, BF16)
    return vmem_call(
        functools.partial(late_kernel, taps),
        [((parts, columns // parts, 128), F32), ((channels * rows, width), F32),
         ((6, rows, width), F32), rim_shape, rim_shape],
        [((6, rows + 32, width), F32), ((6, rows + 32, width), F32),
         ((rows + 2, channels, width), F32), ((128, columns), F32), ((columns, 128), F32)],
        halo_up, halo_dn, frames, cot, wfwd, wbwd, *held)


def both_weights(hw, taps, channels):
    wfwd = order(hw, taps)
    wbwd = wfwd.reshape(128, 3, 3, channels).transpose(1, 3, 2, 0).reshape(3 * channels, 3 * 128)
    return wfwd, wbwd


def fan_kernel(parts_ref, out):
    total = jnp.sum(parts_ref[...], 0).astype(out.dtype)
    for n in range(out.shape[0]):
        out[n] = total


def fan(parts, count, dtype):
    return vmem_call(fan_kernel, [((count,) + parts.shape[1:], dtype)], [], parts)[0]


def unpack(parts, taps, factor):
    count, size, _ = parts.shape
    return vmem_call(
        functools.partial(unpack_kernel, taps, factor),
        [((4 * taps, count * size), F32)], [((count * size, 128), F32)], parts)[0]


PLANE, LINE, TILE = ("y", "core", "x"), ("zl", "zh"), ("x", "zh")


def step(frames, features, cotangent, head_weight):
    taps = head_weight.shape[0] // 4
    rim = (taps - 1) // 2
    feat, frame, cot = features[0], frames[0], cotangent[0]
    channels, rows, width = feat.shape
    tiles, plane, line = lax.axis_size(TILE), lax.axis_size(PLANE), lax.axis_size(LINE)
    down = [(i, i + 1) for i in range(tiles - 1)]
    up = [(i + 1, i) for i in range(tiles - 1)]

    def halo(row, part):
        return jnp.concatenate([feat[:, row], part.reshape(6 * rim, width)], 0)

    halo_up = lax.ppermute(halo(rows - 1, frame[:, :, rows - rim:]), TILE, down)
    halo_dn = lax.ppermute(halo(0, frame[:, :, :rim]), TILE, up)
    wfwd, wbwd = both_weights(head_weight, taps, channels)
    held = early(feat, cot, wfwd, taps)
    parts, gfeat, gframe, rim_up, rim_dn = late(
        halo_up, halo_dn, frame, cot, wfwd, wbwd, held, taps, plane)

    from_up = lax.ppermute(rim_dn, TILE, down)
    from_dn = lax.ppermute(rim_up, TILE, up)

    terms = lax.all_to_all(parts, PLANE, 0, 0)
    terms = lax.all_to_all(fan(terms, line, F32), LINE, 0, 0)
    total = lax.all_to_all(fan(terms, plane, BF16), PLANE, 0, 0)
    from_up, from_dn = from_up.astype(F32), from_dn.astype(F32)
    pixels = plane * line * rows * width
    grad_weight = unpack(total, taps, pixels ** -0.5)

    gfeat = gfeat.reshape(channels, rows, width)
    gfeat = (gfeat + jnp.pad(from_up[:channels, None], ((0, 0), (0, rows - 1), (0, 0)))
             + jnp.pad(from_dn[:channels, None], ((0, 0), (rows - 1, 0), (0, 0))))
    gframe = (gframe
              + jnp.pad(from_up[channels:].reshape(6, rim, width), ((0, 0), (0, rows - rim), (0, 0)))
              + jnp.pad(from_dn[channels:].reshape(6, rim, width), ((0, 0), (rows - rim, 0), (0, 0))))
    return grad_weight, gfeat[None], gframe.reshape(1, 2, 3, rows, width)


def solution(mesh):
    fine = Mesh(mesh.devices.reshape(8, 4, 2, 4, 2), ("zl", "y", "core", "x", "zh"))
    pairs, tile = ("zl", "y", "core"), ("x", "zh")
    in_specs = (
        P(pairs, None, None, tile, None),
        P(pairs, None, tile, None),
        P(pairs, None, tile, None),
        P(),
    )
    out_specs = (P(), P(pairs, None, tile, None), P(pairs, None, None, tile, None))
    return jax.shard_map(step, mesh=fine, in_specs=in_specs, out_specs=out_specs, check_vma=False)
```

```python
import functools
import jax
import jax.numpy as jnp
from jax import lax
from jax.experimental import pallas as pl
from jax.experimental.pallas import tpu as pltpu
from jax.sharding import Mesh, PartitionSpec as P


F32, BF16 = jnp.float32, jnp.bfloat16
UNROLL_EARLY = 7
UNROLL_LATE = 7
UNROLL_FEATURE = 8
GATHER_TYPE = BF16
VMEM_GRANT = 16 * 1024 * 1024


def dims(a, b):
    return (((a,), (b,)), ((), ()))


def split(v):
    hi = v.astype(BF16)
    lo = (v - hi.astype(F32)).astype(BF16)
    return hi, lo


def column_bands(taps, width):
    rim = (taps - 1) // 2
    lane = lax.broadcasted_iota(jnp.int32, (width, width), 1)
    sub = lax.broadcasted_iota(jnp.int32, (width, width), 0)
    bands = []
    for f in range(2):
        tap = (lane - sub + (2 * width - 64 * f)) % width
        at = sub + tap - rim
        bands.append((tap < taps) & (at >= 0) & (at < width))
    return lane, sub, bands


def three_columns(row):
    lane = lax.broadcasted_iota(jnp.int32, row.shape, 1)
    width = row.shape[1]
    left = jnp.where(lane == 0, 0.0, pltpu.roll(row, 1, 1))
    right = jnp.where(lane == width - 1, 0.0, pltpu.roll(row, width - 1, 1))
    return jnp.concatenate([left, row, right], 0).astype(BF16)


def frame_terms(taps, k, g, bands):
    skew = pltpu.roll((k * taps ** -0.5).T, 0, 1, stride=1, stride_axis=0)
    out = []
    for f in range(2):
        v = k[64 * f + 32:64 * f + 64] * taps ** -0.5
        u_hi, u_lo = split(jnp.concatenate([v * g[c] for c in range(3)], 0))
        b_hi, b_lo = split(jnp.where(bands[f], skew, 0.0))
        w = jnp.dot(
            jnp.concatenate([u_hi, u_hi, u_lo], 1),
            jnp.concatenate([b_hi, b_lo, b_hi], 0), preferred_element_type=F32)
        out.append((jnp.concatenate([b_hi, b_lo], 1), jnp.concatenate([u_hi, u_lo], 0), w))
    return out


def early_kernel(taps, feat, frames, cot, wfwd, fb, bst, ust, gf, ip, fs):
    channels, rows, width = feat.shape
    rim = (taps - 1) // 2
    for n in range(6):
        ip[n] = jnp.zeros(ip.shape[1:], F32)
        ip[n, rim:rim + rows] = pltpu.roll(frames[n // 3, n % 3].astype(F32), rim + 64 * (n // 3), 1)
    fs[...] = feat[...].astype(F32).reshape(channels * rows, width)
    for y in range(rows):
        fb[y] = three_columns(fs[pl.ds(y, channels, stride=rows), :])
    gf[...] = jnp.zeros_like(gf)
    _, _, bands = column_bands(taps, width)

    def step(m, carry):
        ya = 2 * m + 1
        pair = jnp.concatenate(
            [fb[pl.ds(ya + h - 1, 3)].reshape(9 * channels, width) for h in range(2)], 1)
        k = jnp.dot(wfwd[...], pair, preferred_element_type=F32)
        for h in range(2):
            y = ya + h
            g = [cot[c, pl.ds(y, 1), :] for c in range(3)]
            terms = frame_terms(taps, k[:, width * h:width * (h + 1)], g, bands)
            for f, (b, u, w) in enumerate(terms):
                bst[y - 1, f] = b
                ust[y - 1, f] = u
                for c in range(3):
                    gf[3 * f + c, pl.ds(y, 32), :] += w[32 * c:32 * c + 32]
        return carry

    lax.fori_loop(0, rows // 2 - 1, step, 0, unroll=UNROLL_EARLY)


def late_kernel(taps, halo_up, halo_dn, cot, wfwd, fb, bst, ust, gf_in, ip_in,
                parts_ref, kgs, gf, ip, wg):
    rim = (taps - 1) // 2
    rows, channels, width = fb.shape[0], fb.shape[1] // 3, fb.shape[2]
    _, sub, bands = column_bands(taps, width)
    head = three_columns(halo_up[:channels].astype(F32))
    foot = three_columns(halo_dn[:channels].astype(F32))
    edges = jnp.concatenate([
        jnp.concatenate([head, fb[0], fb[1]], 0),
        jnp.concatenate([fb[rows - 2], fb[rows - 1], foot], 0)], 1)
    k = jnp.dot(wfwd[...], edges, preferred_element_type=F32)

    ip[...] = ip_in[...]
    for n in range(6):
        at = channels + n * rim
        turn = rim + 64 * (n // 3)
        ip[n, :rim] = pltpu.roll(halo_up[at:at + rim].astype(F32), turn, 1)
        ip[n, rim + rows:rim + rows + rim] = pltpu.roll(halo_dn[at:at + rim].astype(F32), turn, 1)
    gf[...] = gf_in[...]

    def tap_grads(y, terms):
        g = [cot[c, pl.ds(y, 1), :] for c in range(3)]
        grads = []
        horiz = None
        for f, (b, u) in enumerate(terms):
            window = jnp.concatenate(
                [ip[3 * f + c, pl.ds(y, 32), :] for c in range(3)], 0).astype(BF16)
            blended = lax.dot_general(
                jnp.concatenate([window, window], 1), b, dims(1, 1), preferred_element_type=F32)
            grads.append(sum(g[c] * blended[32 * c:32 * c + 32] for c in range(3)))
            d = lax.dot_general(
                u, jnp.concatenate([window, window], 0), dims(0, 0), preferred_element_type=F32)
            horiz = jnp.where(bands[f], d, 0.0 if f == 0 else horiz)
        turned = [horiz[:8]]
        for r in range(1, width // 8):
            turned.append(pltpu.roll(horiz[8 * r:8 * r + 8], width - 8 * r, 1))
        horiz = jnp.concatenate(turned, 0)
        for bit in range(3):
            horiz = jnp.where((sub & (1 << bit)) != 0, pltpu.roll(horiz, width - (1 << bit), 1), horiz)
        ht = horiz.T
        kg = jnp.concatenate([ht[:32], grads[0], ht[64:96], grads[1]], 0) * taps ** -0.5
        kg = kg.astype(BF16)
        kgs[y] = kg
        return kg

    pair_kg = []
    for h, y in enumerate((0, rows - 1)):
        g = [cot[c, y:y + 1, :] for c in range(3)]
        terms = frame_terms(taps, k[:, width * h:width * (h + 1)], g, bands)
        for f, (_, _, w) in enumerate(terms):
            for c in range(3):
                gf[3 * f + c, y:y + 32] += w[32 * c:32 * c + 32]
        pair_kg.append(tap_grads(y, [t[:2] for t in terms]))
    wg[...] = lax.dot_general(
        jnp.concatenate(pair_kg, 1), edges, dims(1, 1), preferred_element_type=F32)

    def step(m, carry):
        ya = 2 * m + 1
        pair = jnp.concatenate(
            [fb[pl.ds(ya + h - 1, 3)].reshape(9 * channels, width) for h in range(2)], 1)
        pair_kg = [
            tap_grads(ya + h, [(bst[ya + h - 1, f], ust[ya + h - 1, f]) for f in range(2)])
            for h in range(2)]
        wg[...] += lax.dot_general(
            jnp.concatenate(pair_kg, 1), pair, dims(1, 1), preferred_element_type=F32)
        return carry

    lax.fori_loop(0, rows // 2 - 1, step, 0, unroll=UNROLL_LATE)
    pack(wg, parts_ref, taps)


def feature_kernel(taps, kgs, gf, wbwd, gfeat, gframe, rim_up, rim_dn, acc, turned):
    rim = (taps - 1) // 2
    rows, _, width = kgs.shape
    channels = acc.shape[1]
    lane = lax.broadcasted_iota(jnp.int32, (128, width), 1)
    acc[...] = jnp.zeros_like(acc)

    def step(m, carry):
        wide = []
        for h in range(2):
            kg = kgs[2 * m + h].astype(F32)
            wide.append(jnp.concatenate([
                jnp.where(lane == width - 1, 0.0, pltpu.roll(kg, width - 1, 1)),
                kg,
                jnp.where(lane == 0, 0.0, pltpu.roll(kg, 1, 1))], 0).astype(BF16))
        part = jnp.dot(wbwd[...], jnp.concatenate(wide, 1), preferred_element_type=F32)
        for h in range(2):
            for a in range(3):
                acc[2 * m + h + a] += part[channels * a:channels * (a + 1), width * h:width * (h + 1)]
        return carry

    lax.fori_loop(0, rows // 2, step, 0, unroll=UNROLL_FEATURE)

    for y in range(rows):
        gfeat[pl.ds(y, channels, stride=rows), :] = acc[y + 1]
    rim_up[:channels] = acc[0].astype(BF16)
    rim_dn[:channels] = acc[rows + 1].astype(BF16)
    for n in range(6):
        turned[...] = pltpu.roll(gf[n], width - rim - 64 * (n // 3), 1)
        gframe[n] = turned[rim:rim + rows]
        at = channels + n * rim
        rim_up[at:at + rim] = turned[:rim].astype(BF16)
        rim_dn[at:at + rim] = turned[rim + rows:rim + rows + rim].astype(BF16)


def pack(wg, parts, taps):
    count, size, _ = parts.shape
    full, high = wg.shape[1] // 128, 4 * taps
    value = jnp.concatenate([wg[32 * g:32 * g + taps] for g in (1, 0, 3, 2)], 0)
    tail = value[:, 128 * full:]
    flat = jnp.concatenate(
        [value[:, 128 * n:128 * (n + 1)] for n in range(full)]
        + [jnp.concatenate([tail[:high // 2], tail[high // 2:]], 1)], 0)
    flat = jnp.concatenate([flat, jnp.zeros((count * size - flat.shape[0], 128), F32)], 0)
    parts[...] = flat.reshape(count, size, 128)


def unpack_kernel(taps, factor, parts, out):
    count, size, _ = parts.shape
    full, high = out.shape[1] // 128, 4 * taps
    flat = parts[...].astype(F32).reshape(count * size, 128) * factor
    for n in range(full):
        out[:, 128 * n:128 * (n + 1)] = flat[high * n:high * (n + 1)]
    tail = flat[high * full:high * full + high // 2]
    out[:, 128 * full:] = jnp.concatenate([tail[:, :64], tail[:, 64:]], 0)


def halo_kernel(taps, feat_hbm, frames_hbm, first, last, feat, frames, fs, sems):
    rim = (taps - 1) // 2
    copies = [pltpu.make_async_copy(feat_hbm, feat, sems.at[0]),
              pltpu.make_async_copy(frames_hbm, frames, sems.at[1])]
    for copy in copies:
        copy.start()
    for copy in copies:
        copy.wait()
    channels, rows, width = feat.shape
    fs[...] = feat[...].astype(F32).reshape(channels * rows, width)
    first[:channels] = fs[pl.ds(0, channels, stride=rows), :].astype(BF16)
    last[:channels] = fs[pl.ds(rows - 1, channels, stride=rows), :].astype(BF16)
    for n in range(6):
        frame = frames[n // 3, n % 3].astype(F32)
        at = channels + n * rim
        first[at:at + rim] = frame[:rim].astype(BF16)
        last[at:at + rim] = frame[rows - rim:].astype(BF16)


def order(hw, taps):
    hw = hw.reshape(2, 2, taps, -1)[:, ::-1]
    return jnp.pad(hw, ((0, 0), (0, 0), (0, 32 - taps), (0, 0))).reshape(128, -1)


def vmem_call(kernel, outs, scratch, *operands):
    vm = pl.BlockSpec(memory_space=pltpu.VMEM)
    return pl.pallas_call(
        kernel,
        out_shape=[jax.ShapeDtypeStruct(*o) for o in outs],
        in_specs=[vm] * len(operands),
        out_specs=[vm] * len(outs),
        scratch_shapes=[pltpu.VMEM(*o) for o in scratch],
        compiler_params=pltpu.CompilerParams(vmem_limit_bytes=VMEM_GRANT),
    )(*operands)


def early(feat, frames, cot, wfwd, taps):
    channels, rows, width = feat.shape
    return vmem_call(
        functools.partial(early_kernel, taps),
        [((rows, 3 * channels, width), BF16), ((rows - 2, 2, width, 2 * width), BF16),
         ((rows - 2, 2, 192, width), BF16), ((6, rows + 32, width), F32), ((6, rows + 32, width), F32)],
        [((channels * rows, width), F32)],
        feat, frames, cot, wfwd)


def late(halo_up, halo_dn, cot, wfwd, held, taps, parts):
    rows, width = held[0].shape[0], held[0].shape[2]
    columns = 3 * held[0].shape[1]
    size = -(-4 * taps * columns // (128 * parts * 8)) * 8
    return vmem_call(
        functools.partial(late_kernel, taps),
        [((parts, size, 128), F32), ((rows, 128, width), BF16), ((6, rows + 32, width), F32)],
        [((6, rows + 32, width), F32), ((128, columns), F32)],
        halo_up, halo_dn, cot, wfwd, *held)


def feature_part(kgs, gf, wbwd, taps):
    rows, _, width = kgs.shape
    channels = wbwd.shape[0] // 3
    rim_shape = ((channels + 3 * (taps - 1), width), BF16)
    return vmem_call(
        functools.partial(feature_kernel, taps),
        [((channels * rows, width), F32), ((6, rows, width), F32), rim_shape, rim_shape],
        [((rows + 2, channels, width), F32), (gf.shape[1:], F32)],
        kgs, gf, wbwd)


def halo_rows(feat, frames, taps):
    channels, rows, width = feat.shape
    shape = ((channels + 3 * (taps - 1), width), BF16)
    hbm, vm = pl.BlockSpec(memory_space=pltpu.HBM), pl.BlockSpec(memory_space=pltpu.VMEM)
    return pl.pallas_call(
        functools.partial(halo_kernel, taps),
        out_shape=[jax.ShapeDtypeStruct(*shape)] * 2,
        in_specs=[hbm, hbm],
        out_specs=[vm, vm],
        scratch_shapes=[pltpu.VMEM(feat.shape, BF16), pltpu.VMEM(frames.shape, BF16),
                        pltpu.VMEM((channels * rows, width), F32), pltpu.SemaphoreType.DMA((2,))],
    )(feat, frames)


def both_weights(hw, taps, channels):
    wfwd = order(hw, taps)
    wbwd = wfwd.reshape(128, 3, 3, channels).transpose(1, 3, 2, 0).reshape(3 * channels, 3 * 128)
    return wfwd, wbwd


def fan_kernel(parts_ref, out):
    total = jnp.sum(parts_ref[...], 0).astype(out.dtype)
    for n in range(out.shape[0]):
        out[n] = total


def fan(parts, count, dtype):
    return vmem_call(fan_kernel, [((count,) + parts.shape[1:], dtype)], [], parts)[0]


def unpack(parts, taps, columns, factor):
    return vmem_call(
        functools.partial(unpack_kernel, taps, factor), [((4 * taps, columns), F32)], [], parts)[0]


PLANE, LINE, TILE = ("y", "core", "x"), ("zl", "zh"), ("x", "zh")


def step(frames, features, cotangent, head_weight):
    taps = head_weight.shape[0] // 4
    rim = (taps - 1) // 2
    feat, frame, cot = features[0], frames[0], cotangent[0]
    channels, rows, width = feat.shape
    tiles, plane, line = lax.axis_size(TILE), lax.axis_size(PLANE), lax.axis_size(LINE)
    down = [(i, i + 1) for i in range(tiles - 1)]
    up = [(i + 1, i) for i in range(tiles - 1)]

    first, last = halo_rows(feat, frame, taps)
    halo_up = lax.ppermute(last, TILE, down)
    halo_dn = lax.ppermute(first, TILE, up)
    wfwd, wbwd = both_weights(head_weight, taps, channels)
    held = early(feat, frame, cot, wfwd, taps)
    parts, kgs, gf = late(halo_up, halo_dn, cot, wfwd, held, taps, plane)

    terms = lax.all_to_all(parts, PLANE, 0, 0)
    gfeat, gframe, rim_up, rim_dn = feature_part(kgs, gf, wbwd, taps)
    from_up = lax.ppermute(rim_dn, TILE, down)
    from_dn = lax.ppermute(rim_up, TILE, up)
    terms = lax.all_to_all(fan(terms, line, F32), LINE, 0, 0)
    total = lax.all_to_all(fan(terms, plane, GATHER_TYPE), PLANE, 0, 0)
    from_up, from_dn = from_up.astype(F32), from_dn.astype(F32)
    pixels = plane * line * rows * width
    grad_weight = unpack(total, taps, 9 * channels, pixels ** -0.5)

    gfeat = gfeat.reshape(channels, rows, width)
    gfeat = (gfeat + jnp.pad(from_up[:channels, None], ((0, 0), (0, rows - 1), (0, 0)))
             + jnp.pad(from_dn[:channels, None], ((0, 0), (rows - 1, 0), (0, 0))))
    gframe = (gframe
              + jnp.pad(from_up[channels:].reshape(6, rim, width), ((0, 0), (0, rows - rim), (0, 0)))
              + jnp.pad(from_dn[channels:].reshape(6, rim, width), ((0, 0), (rows - rim, 0), (0, 0))))
    return grad_weight, gfeat[None], gframe.reshape(1, 2, 3, rows, width)


def solution(mesh):
    fine = Mesh(mesh.devices.reshape(8, 4, 2, 4, 2), ("zl", "y", "core", "x", "zh"))
    pairs, tile = ("zl", "y", "core"), ("x", "zh")
    in_specs = (
        P(pairs, None, None, tile, None),
        P(pairs, None, tile, None),
        P(pairs, None, tile, None),
        P(),
    )
    out_specs = (P(), P(pairs, None, tile, None), P(pairs, None, None, tile, None))
    return jax.shard_map(step, mesh=fine, in_specs=in_specs, out_specs=out_specs, check_vma=False)
```

```python
import functools
import jax
import jax.numpy as jnp
from jax import lax
from jax.experimental import pallas as pl
from jax.experimental.pallas import tpu as pltpu
from jax.sharding import Mesh, PartitionSpec as P


F32, BF16 = jnp.float32, jnp.bfloat16
UNROLL_EARLY = 7
UNROLL_LATE = 7
UNROLL_FEATURE = 8
GATHER_TYPE = BF16
VMEM_GRANT = 16 * 1024 * 1024


def dims(a, b):
    return (((a,), (b,)), ((), ()))


def split(v):
    hi = v.astype(BF16)
    lo = (v - hi.astype(F32)).astype(BF16)
    return hi, lo


def column_bands(taps, width):
    rim = (taps - 1) // 2
    lane = lax.broadcasted_iota(jnp.int32, (width, width), 1)
    sub = lax.broadcasted_iota(jnp.int32, (width, width), 0)
    bands = []
    for f in range(2):
        tap = (lane - sub + (2 * width - 64 * f)) % width
        at = sub + tap - rim
        bands.append((tap < taps) & (at >= 0) & (at < width))
    return lane, sub, bands


def three_columns(row):
    lane = lax.broadcasted_iota(jnp.int32, row.shape, 1)
    width = row.shape[1]
    left = jnp.where(lane == 0, 0.0, pltpu.roll(row, 1, 1))
    right = jnp.where(lane == width - 1, 0.0, pltpu.roll(row, width - 1, 1))
    return jnp.concatenate([left, row, right], 0).astype(BF16)


def frame_terms(taps, k, g, bands):
    skew = pltpu.roll((k * taps ** -0.5).T, 0, 1, stride=1, stride_axis=0)
    out = []
    for f in range(2):
        v = k[64 * f + 32:64 * f + 64] * taps ** -0.5
        u_hi, u_lo = split(jnp.concatenate([v * g[c] for c in range(3)], 0))
        b_hi, b_lo = split(jnp.where(bands[f], skew, 0.0))
        w = jnp.dot(
            jnp.concatenate([u_hi, u_hi, u_lo], 1),
            jnp.concatenate([b_hi, b_lo, b_hi], 0), preferred_element_type=F32)
        out.append((jnp.concatenate([b_hi, b_lo], 1), jnp.concatenate([u_hi, u_lo], 0), w))
    return out


def early_kernel(taps, feat, frames, cot, wfwd, fb, bst, ust, gf, ip, fs):
    channels, rows, width = feat.shape
    rim = (taps - 1) // 2
    for n in range(6):
        ip[n] = jnp.zeros(ip.shape[1:], F32)
        ip[n, rim:rim + rows] = pltpu.roll(frames[n // 3, n % 3].astype(F32), rim + 64 * (n // 3), 1)
    fs[...] = feat[...].astype(F32).reshape(channels * rows, width)
    for y in range(rows):
        fb[y] = three_columns(fs[pl.ds(y, channels, stride=rows), :])
    gf[...] = jnp.zeros_like(gf)
    _, _, bands = column_bands(taps, width)

    def step(m, carry):
        ya = 2 * m + 1
        pair = jnp.concatenate(
            [fb[pl.ds(ya + h - 1, 3)].reshape(9 * channels, width) for h in range(2)], 1)
        k = jnp.dot(wfwd[...], pair, preferred_element_type=F32)
        for h in range(2):
            y = ya + h
            g = [cot[c, pl.ds(y, 1), :] for c in range(3)]
            terms = frame_terms(taps, k[:, width * h:width * (h + 1)], g, bands)
            for f, (b, u, w) in enumerate(terms):
                bst[y - 1, f] = b
                ust[y - 1, f] = u
                for c in range(3):
                    gf[3 * f + c, pl.ds(y, 32), :] += w[32 * c:32 * c + 32]
        return carry

    lax.fori_loop(0, rows // 2 - 1, step, 0, unroll=UNROLL_EARLY)


def late_kernel(taps, halo_up, halo_dn, cot, wfwd, fb, bst, ust, gf_in, ip_in,
                parts_ref, kgs, gf, ip, wg):
    rim = (taps - 1) // 2
    rows, channels, width = fb.shape[0], fb.shape[1] // 3, fb.shape[2]
    _, sub, bands = column_bands(taps, width)
    head = three_columns(halo_up[:channels].astype(F32))
    foot = three_columns(halo_dn[:channels].astype(F32))
    edges = jnp.concatenate([
        jnp.concatenate([head, fb[0], fb[1]], 0),
        jnp.concatenate([fb[rows - 2], fb[rows - 1], foot], 0)], 1)
    k = jnp.dot(wfwd[...], edges, preferred_element_type=F32)

    ip[...] = ip_in[...]
    for n in range(6):
        at = channels + n * rim
        turn = rim + 64 * (n // 3)
        ip[n, :rim] = pltpu.roll(halo_up[at:at + rim].astype(F32), turn, 1)
        ip[n, rim + rows:rim + rows + rim] = pltpu.roll(halo_dn[at:at + rim].astype(F32), turn, 1)
    gf[...] = gf_in[...]

    def tap_grads(y, terms):
        g = [cot[c, pl.ds(y, 1), :] for c in range(3)]
        grads = []
        horiz = None
        for f, (b, u) in enumerate(terms):
            window = jnp.concatenate(
                [ip[3 * f + c, pl.ds(y, 32), :] for c in range(3)], 0).astype(BF16)
            blended = lax.dot_general(
                jnp.concatenate([window, window], 1), b, dims(1, 1), preferred_element_type=F32)
            grads.append(sum(g[c] * blended[32 * c:32 * c + 32] for c in range(3)))
            d = lax.dot_general(
                u, jnp.concatenate([window, window], 0), dims(0, 0), preferred_element_type=F32)
            horiz = jnp.where(bands[f], d, 0.0 if f == 0 else horiz)
        turned = [horiz[:8]]
        for r in range(1, width // 8):
            turned.append(pltpu.roll(horiz[8 * r:8 * r + 8], width - 8 * r, 1))
        horiz = jnp.concatenate(turned, 0)
        for bit in range(3):
            horiz = jnp.where((sub & (1 << bit)) != 0, pltpu.roll(horiz, width - (1 << bit), 1), horiz)
        ht = horiz.T
        kg = jnp.concatenate([ht[:32], grads[0], ht[64:96], grads[1]], 0) * taps ** -0.5
        kg = kg.astype(BF16)
        kgs[y] = kg
        return kg

    pair_kg = []
    for h, y in enumerate((0, rows - 1)):
        g = [cot[c, y:y + 1, :] for c in range(3)]
        terms = frame_terms(taps, k[:, width * h:width * (h + 1)], g, bands)
        for f, (_, _, w) in enumerate(terms):
            for c in range(3):
                gf[3 * f + c, y:y + 32] += w[32 * c:32 * c + 32]
        pair_kg.append(tap_grads(y, [t[:2] for t in terms]))
    wg[...] = lax.dot_general(
        jnp.concatenate(pair_kg, 1), edges, dims(1, 1), preferred_element_type=F32)

    def step(m, carry):
        ya = 2 * m + 1
        pair = jnp.concatenate(
            [fb[pl.ds(ya + h - 1, 3)].reshape(9 * channels, width) for h in range(2)], 1)
        pair_kg = [
            tap_grads(ya + h, [(bst[ya + h - 1, f], ust[ya + h - 1, f]) for f in range(2)])
            for h in range(2)]
        wg[...] += lax.dot_general(
            jnp.concatenate(pair_kg, 1), pair, dims(1, 1), preferred_element_type=F32)
        return carry

    lax.fori_loop(0, rows // 2 - 1, step, 0, unroll=UNROLL_LATE)
    pack(wg, parts_ref, taps)


def feature_kernel(taps, half, kgs, gf, wbwd, gfeat, gframe, rims, acc, turned):
    rim = (taps - 1) // 2
    rows, _, width = kgs.shape
    channels = acc.shape[1]
    lane = lax.broadcasted_iota(jnp.int32, (128, width), 1)
    acc[...] = jnp.zeros_like(acc)

    def step(m, carry):
        wide = []
        for h in range(2):
            kg = kgs[2 * m + h].astype(F32)
            wide.append(jnp.concatenate([
                jnp.where(lane == width - 1, 0.0, pltpu.roll(kg, width - 1, 1)),
                kg,
                jnp.where(lane == 0, 0.0, pltpu.roll(kg, 1, 1))], 0).astype(BF16))
        part = jnp.dot(wbwd[...], jnp.concatenate(wide, 1), preferred_element_type=F32)
        for h in range(2):
            for a in range(3):
                acc[2 * m + h + a] += part[channels * a:channels * (a + 1), width * h:width * (h + 1)]
        return carry

    lax.fori_loop(0, rows // 2, step, 0, unroll=UNROLL_FEATURE)

    for y in range(rows):
        gfeat[pl.ds(y, channels, stride=rows), :] = acc[y + 1]
    up, dn = 1 - half[0], half[0]
    rims[up, :channels] = acc[0].astype(BF16)
    rims[dn, :channels] = acc[rows + 1].astype(BF16)
    for n in range(6):
        turned[...] = pltpu.roll(gf[n], width - rim - 64 * (n // 3), 1)
        gframe[n] = turned[rim:rim + rows]
        at = channels + n * rim
        rims[up, at:at + rim] = turned[:rim].astype(BF16)
        rims[dn, at:at + rim] = turned[rim + rows:rim + rows + rim].astype(BF16)


def pack(wg, parts, taps):
    count, size, _ = parts.shape
    full, high = wg.shape[1] // 128, 4 * taps
    value = jnp.concatenate([wg[32 * g:32 * g + taps] for g in (1, 0, 3, 2)], 0)
    tail = value[:, 128 * full:]
    flat = jnp.concatenate(
        [value[:, 128 * n:128 * (n + 1)] for n in range(full)]
        + [jnp.concatenate([tail[:high // 2], tail[high // 2:]], 1)], 0)
    flat = jnp.concatenate([flat, jnp.zeros((count * size - flat.shape[0], 128), F32)], 0)
    parts[...] = flat.reshape(count, size, 128)


def unpack_kernel(taps, factor, parts, out):
    count, size, _ = parts.shape
    full, high = out.shape[1] // 128, 4 * taps
    flat = parts[...].astype(F32).reshape(count * size, 128) * factor
    for n in range(full):
        out[:, 128 * n:128 * (n + 1)] = flat[high * n:high * (n + 1)]
    tail = flat[high * full:high * full + high // 2]
    out[:, 128 * full:] = jnp.concatenate([tail[:, :64], tail[:, 64:]], 0)


def halo_kernel(taps, feat_hbm, frames_hbm, first, last, feat, frames, fs, sems):
    rim = (taps - 1) // 2
    copies = [pltpu.make_async_copy(feat_hbm, feat, sems.at[0]),
              pltpu.make_async_copy(frames_hbm, frames, sems.at[1])]
    for copy in copies:
        copy.start()
    for copy in copies:
        copy.wait()
    channels, rows, width = feat.shape
    fs[...] = feat[...].astype(F32).reshape(channels * rows, width)
    first[:channels] = fs[pl.ds(0, channels, stride=rows), :].astype(BF16)
    last[:channels] = fs[pl.ds(rows - 1, channels, stride=rows), :].astype(BF16)
    for n in range(6):
        frame = frames[n // 3, n % 3].astype(F32)
        at = channels + n * rim
        first[at:at + rim] = frame[:rim].astype(BF16)
        last[at:at + rim] = frame[rows - rim:].astype(BF16)


def order(hw, taps):
    hw = hw.reshape(2, 2, taps, -1)[:, ::-1]
    return jnp.pad(hw, ((0, 0), (0, 0), (0, 32 - taps), (0, 0))).reshape(128, -1)


def vmem_call(kernel, outs, scratch, *operands):
    vm = pl.BlockSpec(memory_space=pltpu.VMEM)
    return pl.pallas_call(
        kernel,
        out_shape=[jax.ShapeDtypeStruct(*o) for o in outs],
        in_specs=[vm] * len(operands),
        out_specs=[vm] * len(outs),
        scratch_shapes=[pltpu.VMEM(*o) for o in scratch],
        compiler_params=pltpu.CompilerParams(vmem_limit_bytes=VMEM_GRANT),
    )(*operands)


def early(feat, frames, cot, wfwd, taps):
    channels, rows, width = feat.shape
    return vmem_call(
        functools.partial(early_kernel, taps),
        [((rows, 3 * channels, width), BF16), ((rows - 2, 2, width, 2 * width), BF16),
         ((rows - 2, 2, 192, width), BF16), ((6, rows + 32, width), F32), ((6, rows + 32, width), F32)],
        [((channels * rows, width), F32)],
        feat, frames, cot, wfwd)


def late(halo_up, halo_dn, cot, wfwd, held, taps, parts):
    rows, width = held[0].shape[0], held[0].shape[2]
    columns = 3 * held[0].shape[1]
    size = -(-4 * taps * columns // (128 * parts * 8)) * 8
    return vmem_call(
        functools.partial(late_kernel, taps),
        [((parts, size, 128), F32), ((rows, 128, width), BF16), ((6, rows + 32, width), F32)],
        [((6, rows + 32, width), F32), ((128, columns), F32)],
        halo_up, halo_dn, cot, wfwd, *held)


def feature_part(half, kgs, gf, wbwd, taps):
    rows, _, width = kgs.shape
    channels = wbwd.shape[0] // 3
    vm = pl.BlockSpec(memory_space=pltpu.VMEM)
    return pl.pallas_call(
        functools.partial(feature_kernel, taps),
        out_shape=[jax.ShapeDtypeStruct((channels * rows, width), F32),
                   jax.ShapeDtypeStruct((6, rows, width), F32),
                   jax.ShapeDtypeStruct((2, channels + 3 * (taps - 1), width), BF16)],
        in_specs=[pl.BlockSpec(memory_space=pltpu.SMEM), vm, vm, vm],
        out_specs=[vm] * 3,
        scratch_shapes=[pltpu.VMEM((rows + 2, channels, width), F32), pltpu.VMEM(gf.shape[1:], F32)],
        compiler_params=pltpu.CompilerParams(vmem_limit_bytes=VMEM_GRANT),
    )(half, kgs, gf, wbwd)


def halo_rows(feat, frames, taps):
    channels, rows, width = feat.shape
    shape = ((channels + 3 * (taps - 1), width), BF16)
    hbm, vm = pl.BlockSpec(memory_space=pltpu.HBM), pl.BlockSpec(memory_space=pltpu.VMEM)
    return pl.pallas_call(
        functools.partial(halo_kernel, taps),
        out_shape=[jax.ShapeDtypeStruct(*shape)] * 2,
        in_specs=[hbm, hbm],
        out_specs=[vm, vm],
        scratch_shapes=[pltpu.VMEM(feat.shape, BF16), pltpu.VMEM(frames.shape, BF16),
                        pltpu.VMEM((channels * rows, width), F32), pltpu.SemaphoreType.DMA((2,))],
    )(feat, frames)


def both_weights(hw, taps, channels):
    wfwd = order(hw, taps)
    wbwd = wfwd.reshape(128, 3, 3, channels).transpose(1, 3, 2, 0).reshape(3 * channels, 3 * 128)
    return wfwd, wbwd


def fan_kernel(parts_ref, out):
    total = jnp.sum(parts_ref[...], 0).astype(out.dtype)
    for n in range(out.shape[0]):
        out[n] = total


def fan(parts, count, dtype):
    return vmem_call(fan_kernel, [((count,) + parts.shape[1:], dtype)], [], parts)[0]


def unpack(parts, taps, columns, factor):
    return vmem_call(
        functools.partial(unpack_kernel, taps, factor), [((4 * taps, columns), F32)], [], parts)[0]


PLANE, LINE, TILE = ("y", "core", "x"), ("zl", "zh"), ("x", "zh")


def step(frames, features, cotangent, head_weight):
    taps = head_weight.shape[0] // 4
    rim = (taps - 1) // 2
    feat, frame, cot = features[0], frames[0], cotangent[0]
    channels, rows, width = feat.shape
    tiles, plane, line = lax.axis_size(TILE), lax.axis_size(PLANE), lax.axis_size(LINE)
    down = [(i, i + 1) for i in range(tiles - 1)]
    up = [(i + 1, i) for i in range(tiles - 1)]

    first, last = halo_rows(feat, frame, taps)
    halo_up = lax.ppermute(last, TILE, down)
    halo_dn = lax.ppermute(first, TILE, up)
    wfwd, wbwd = both_weights(head_weight, taps, channels)
    held = early(feat, frame, cot, wfwd, taps)
    parts, kgs, gf = late(halo_up, halo_dn, cot, wfwd, held, taps, plane)

    terms = lax.all_to_all(parts, PLANE, 0, 0)
    half = lax.axis_index("zh")
    gfeat, gframe, rims = feature_part(half.reshape(1), kgs, gf, wbwd, taps)
    rims = lax.ppermute(rims, TILE, [(i, i ^ 1) for i in range(tiles)])
    near = rims[0]
    far = lax.ppermute(rims[1], TILE, [(i, i + 2) for i in range(0, tiles - 2, 2)]
                       + [(i, i - 2) for i in range(3, tiles, 2)])
    terms = lax.all_to_all(fan(terms, line, F32), LINE, 0, 0)
    total = lax.all_to_all(fan(terms, plane, GATHER_TYPE), PLANE, 0, 0)
    from_up = jnp.where(half == 0, far, near).astype(F32)
    from_dn = jnp.where(half == 0, near, far).astype(F32)
    pixels = plane * line * rows * width
    grad_weight = unpack(total, taps, 9 * channels, pixels ** -0.5)

    gfeat = gfeat.reshape(channels, rows, width)
    gfeat = (gfeat + jnp.pad(from_up[:channels, None], ((0, 0), (0, rows - 1), (0, 0)))
             + jnp.pad(from_dn[:channels, None], ((0, 0), (rows - 1, 0), (0, 0))))
    gframe = (gframe
              + jnp.pad(from_up[channels:].reshape(6, rim, width), ((0, 0), (0, rows - rim), (0, 0)))
              + jnp.pad(from_dn[channels:].reshape(6, rim, width), ((0, 0), (rows - rim, 0), (0, 0))))
    return grad_weight, gfeat[None], gframe.reshape(1, 2, 3, rows, width)


def solution(mesh):
    fine = Mesh(mesh.devices.reshape(8, 4, 2, 4, 2), ("zl", "y", "core", "x", "zh"))
    pairs, tile = ("zl", "y", "core"), ("x", "zh")
    in_specs = (
        P(pairs, None, None, tile, None),
        P(pairs, None, tile, None),
        P(pairs, None, tile, None),
        P(),
    )
    out_specs = (P(), P(pairs, None, tile, None), P(pairs, None, None, tile, None))
    return jax.shard_map(step, mesh=fine, in_specs=in_specs, out_specs=out_specs, check_vma=False)
```

```python
import functools
import jax
import jax.numpy as jnp
from jax import lax
from jax.experimental import pallas as pl
from jax.experimental.pallas import tpu as pltpu
from jax.sharding import Mesh, PartitionSpec as P


F32, BF16 = jnp.float32, jnp.bfloat16
UNROLL_EARLY = 7
UNROLL_LATE = 7
UNROLL_FEATURE = 8
GATHER_TYPE = BF16
VMEM_GRANT = 16 * 1024 * 1024


def dims(a, b):
    return (((a,), (b,)), ((), ()))


def split(v):
    hi = v.astype(BF16)
    lo = (v - hi.astype(F32)).astype(BF16)
    return hi, lo


def column_bands(taps, width):
    rim = (taps - 1) // 2
    lane = lax.broadcasted_iota(jnp.int32, (width, width), 1)
    sub = lax.broadcasted_iota(jnp.int32, (width, width), 0)
    bands = []
    for f in range(2):
        tap = (lane - sub + (2 * width - 64 * f)) % width
        at = sub + tap - rim
        bands.append((tap < taps) & (at >= 0) & (at < width))
    return lane, sub, bands


def three_columns(row):
    lane = lax.broadcasted_iota(jnp.int32, row.shape, 1)
    width = row.shape[1]
    left = jnp.where(lane == 0, 0.0, pltpu.roll(row, 1, 1))
    right = jnp.where(lane == width - 1, 0.0, pltpu.roll(row, width - 1, 1))
    return jnp.concatenate([left, row, right], 0).astype(BF16)


def frame_terms(taps, k, g, bands):
    skew = pltpu.roll((k * taps ** -0.5).T, 0, 1, stride=1, stride_axis=0)
    out = []
    for f in range(2):
        v = k[64 * f + 32:64 * f + 64] * taps ** -0.5
        u_hi, u_lo = split(jnp.concatenate([v * g[c] for c in range(3)], 0))
        b_hi, b_lo = split(jnp.where(bands[f], skew, 0.0))
        w = jnp.dot(
            jnp.concatenate([u_hi, u_hi, u_lo], 1),
            jnp.concatenate([b_hi, b_lo, b_hi], 0), preferred_element_type=F32)
        out.append((jnp.concatenate([b_hi, b_lo], 1), jnp.concatenate([u_hi, u_lo], 0), w))
    return out


def early_kernel(taps, feat, frames, cot, wfwd, fb, bst, ust, gf, ip, fs):
    channels, rows, width = feat.shape
    rim = (taps - 1) // 2
    for n in range(6):
        ip[n] = jnp.zeros(ip.shape[1:], F32)
        ip[n, rim:rim + rows] = pltpu.roll(frames[n // 3, n % 3].astype(F32), rim + 64 * (n // 3), 1)
    fs[...] = feat[...].astype(F32).reshape(channels * rows, width)
    for y in range(rows):
        fb[y] = three_columns(fs[pl.ds(y, channels, stride=rows), :])
    gf[...] = jnp.zeros_like(gf)
    _, _, bands = column_bands(taps, width)

    def step(m, carry):
        ya = 2 * m + 1
        pair = jnp.concatenate(
            [fb[pl.ds(ya + h - 1, 3)].reshape(9 * channels, width) for h in range(2)], 1)
        k = jnp.dot(wfwd[...], pair, preferred_element_type=F32)
        for h in range(2):
            y = ya + h
            g = [cot[c, pl.ds(y, 1), :] for c in range(3)]
            terms = frame_terms(taps, k[:, width * h:width * (h + 1)], g, bands)
            for f, (b, u, w) in enumerate(terms):
                bst[y - 1, f] = b
                ust[y - 1, f] = u
                for c in range(3):
                    gf[3 * f + c, pl.ds(y, 32), :] += w[32 * c:32 * c + 32]
        return carry

    lax.fori_loop(0, rows // 2 - 1, step, 0, unroll=UNROLL_EARLY)


def late_kernel(taps, halo_up, halo_dn, cot, wfwd, fb, bst, ust, gf_in, ip_in,
                parts_ref, kgs, gf, ip, wg):
    rim = (taps - 1) // 2
    rows, channels, width = fb.shape[0], fb.shape[1] // 3, fb.shape[2]
    _, sub, bands = column_bands(taps, width)
    head = three_columns(halo_up[:channels].astype(F32))
    foot = three_columns(halo_dn[:channels].astype(F32))
    edges = jnp.concatenate([
        jnp.concatenate([head, fb[0], fb[1]], 0),
        jnp.concatenate([fb[rows - 2], fb[rows - 1], foot], 0)], 1)
    k = jnp.dot(wfwd[...], edges, preferred_element_type=F32)

    ip[...] = ip_in[...]
    for n in range(6):
        at = channels + n * rim
        turn = rim + 64 * (n // 3)
        ip[n, :rim] = pltpu.roll(halo_up[at:at + rim].astype(F32), turn, 1)
        ip[n, rim + rows:rim + rows + rim] = pltpu.roll(halo_dn[at:at + rim].astype(F32), turn, 1)
    gf[...] = gf_in[...]

    def tap_grads(y, terms):
        g = [cot[c, pl.ds(y, 1), :] for c in range(3)]
        grads = []
        horiz = None
        for f, (b, u) in enumerate(terms):
            window = jnp.concatenate(
                [ip[3 * f + c, pl.ds(y, 32), :] for c in range(3)], 0).astype(BF16)
            blended = lax.dot_general(
                jnp.concatenate([window, window], 1), b, dims(1, 1), preferred_element_type=F32)
            grads.append(sum(g[c] * blended[32 * c:32 * c + 32] for c in range(3)))
            d = lax.dot_general(
                u, jnp.concatenate([window, window], 0), dims(0, 0), preferred_element_type=F32)
            horiz = jnp.where(bands[f], d, 0.0 if f == 0 else horiz)
        turned = [horiz[:8]]
        for r in range(1, width // 8):
            turned.append(pltpu.roll(horiz[8 * r:8 * r + 8], width - 8 * r, 1))
        horiz = jnp.concatenate(turned, 0)
        for bit in range(3):
            horiz = jnp.where((sub & (1 << bit)) != 0, pltpu.roll(horiz, width - (1 << bit), 1), horiz)
        ht = horiz.T
        kg = jnp.concatenate([ht[:32], grads[0], ht[64:96], grads[1]], 0) * taps ** -0.5
        kg = kg.astype(BF16)
        kgs[y] = kg
        return kg

    pair_kg = []
    for h, y in enumerate((0, rows - 1)):
        g = [cot[c, y:y + 1, :] for c in range(3)]
        terms = frame_terms(taps, k[:, width * h:width * (h + 1)], g, bands)
        for f, (_, _, w) in enumerate(terms):
            for c in range(3):
                gf[3 * f + c, y:y + 32] += w[32 * c:32 * c + 32]
        pair_kg.append(tap_grads(y, [t[:2] for t in terms]))
    wg[...] = lax.dot_general(
        jnp.concatenate(pair_kg, 1), edges, dims(1, 1), preferred_element_type=F32)

    def step(m, carry):
        ya = 2 * m + 1
        pair = jnp.concatenate(
            [fb[pl.ds(ya + h - 1, 3)].reshape(9 * channels, width) for h in range(2)], 1)
        pair_kg = [
            tap_grads(ya + h, [(bst[ya + h - 1, f], ust[ya + h - 1, f]) for f in range(2)])
            for h in range(2)]
        wg[...] += lax.dot_general(
            jnp.concatenate(pair_kg, 1), pair, dims(1, 1), preferred_element_type=F32)
        return carry

    lax.fori_loop(0, rows // 2 - 1, step, 0, unroll=UNROLL_LATE)
    pack(wg, parts_ref, taps)


def feature_kernel(taps, half, kgs, gf, wbwd, gfeat, gframe, near, far, acc, turned, rims):
    rim = (taps - 1) // 2
    rows, _, width = kgs.shape
    channels = acc.shape[1]
    lane = lax.broadcasted_iota(jnp.int32, (128, width), 1)
    acc[...] = jnp.zeros_like(acc)

    def step(m, carry):
        wide = []
        for h in range(2):
            kg = kgs[2 * m + h].astype(F32)
            wide.append(jnp.concatenate([
                jnp.where(lane == width - 1, 0.0, pltpu.roll(kg, width - 1, 1)),
                kg,
                jnp.where(lane == 0, 0.0, pltpu.roll(kg, 1, 1))], 0).astype(BF16))
        part = jnp.dot(wbwd[...], jnp.concatenate(wide, 1), preferred_element_type=F32)
        for h in range(2):
            for a in range(3):
                acc[2 * m + h + a] += part[channels * a:channels * (a + 1), width * h:width * (h + 1)]
        return carry

    lax.fori_loop(0, rows // 2, step, 0, unroll=UNROLL_FEATURE)

    for y in range(rows):
        gfeat[pl.ds(y, channels, stride=rows), :] = acc[y + 1]
    up, dn = 1 - half[0], half[0]
    rims[up, :channels] = acc[0].astype(BF16)
    rims[dn, :channels] = acc[rows + 1].astype(BF16)
    for n in range(6):
        turned[...] = pltpu.roll(gf[n], width - rim - 64 * (n // 3), 1)
        gframe[n] = turned[rim:rim + rows]
        at = channels + n * rim
        rims[up, at:at + rim] = turned[:rim].astype(BF16)
        rims[dn, at:at + rim] = turned[rim + rows:rim + rows + rim].astype(BF16)
    near[...] = rims[0]
    far[...] = rims[1]


def pack(wg, parts, taps):
    count, size, _ = parts.shape
    full, high = wg.shape[1] // 128, 4 * taps
    value = jnp.concatenate([wg[32 * g:32 * g + taps] for g in (1, 0, 3, 2)], 0)
    tail = value[:, 128 * full:]
    flat = jnp.concatenate(
        [value[:, 128 * n:128 * (n + 1)] for n in range(full)]
        + [jnp.concatenate([tail[:high // 2], tail[high // 2:]], 1)], 0)
    flat = jnp.concatenate([flat, jnp.zeros((count * size - flat.shape[0], 128), F32)], 0)
    parts[...] = flat.reshape(count, size, 128)


def unpack_kernel(taps, factor, parts, out):
    count, size, _ = parts.shape
    full, high = out.shape[1] // 128, 4 * taps
    flat = parts[...].astype(F32).reshape(count * size, 128) * factor
    for n in range(full):
        out[:, 128 * n:128 * (n + 1)] = flat[high * n:high * (n + 1)]
    tail = flat[high * full:high * full + high // 2]
    out[:, 128 * full:] = jnp.concatenate([tail[:, :64], tail[:, 64:]], 0)


def halo_kernel(taps, feat_hbm, frames_hbm, first, last, feat, frames, fs, sems):
    rim = (taps - 1) // 2
    copies = [pltpu.make_async_copy(feat_hbm, feat, sems.at[0]),
              pltpu.make_async_copy(frames_hbm, frames, sems.at[1])]
    for copy in copies:
        copy.start()
    for copy in copies:
        copy.wait()
    channels, rows, width = feat.shape
    fs[...] = feat[...].astype(F32).reshape(channels * rows, width)
    first[:channels] = fs[pl.ds(0, channels, stride=rows), :].astype(BF16)
    last[:channels] = fs[pl.ds(rows - 1, channels, stride=rows), :].astype(BF16)
    for n in range(6):
        frame = frames[n // 3, n % 3].astype(F32)
        at = channels + n * rim
        first[at:at + rim] = frame[:rim].astype(BF16)
        last[at:at + rim] = frame[rows - rim:].astype(BF16)


def order(hw, taps):
    hw = hw.reshape(2, 2, taps, -1)[:, ::-1]
    return jnp.pad(hw, ((0, 0), (0, 0), (0, 32 - taps), (0, 0))).reshape(128, -1)


def vmem_call(kernel, outs, scratch, *operands):
    vm = pl.BlockSpec(memory_space=pltpu.VMEM)
    return pl.pallas_call(
        kernel,
        out_shape=[jax.ShapeDtypeStruct(*o) for o in outs],
        in_specs=[vm] * len(operands),
        out_specs=[vm] * len(outs),
        scratch_shapes=[pltpu.VMEM(*o) for o in scratch],
        compiler_params=pltpu.CompilerParams(vmem_limit_bytes=VMEM_GRANT),
    )(*operands)


def early(feat, frames, cot, wfwd, taps):
    channels, rows, width = feat.shape
    return vmem_call(
        functools.partial(early_kernel, taps),
        [((rows, 3 * channels, width), BF16), ((rows - 2, 2, width, 2 * width), BF16),
         ((rows - 2, 2, 192, width), BF16), ((6, rows + 32, width), F32), ((6, rows + 32, width), F32)],
        [((channels * rows, width), F32)],
        feat, frames, cot, wfwd)


def late(halo_up, halo_dn, cot, wfwd, held, taps, parts):
    rows, width = held[0].shape[0], held[0].shape[2]
    columns = 3 * held[0].shape[1]
    size = -(-4 * taps * columns // (128 * parts * 8)) * 8
    return vmem_call(
        functools.partial(late_kernel, taps),
        [((parts, size, 128), F32), ((rows, 128, width), BF16), ((6, rows + 32, width), F32)],
        [((6, rows + 32, width), F32), ((128, columns), F32)],
        halo_up, halo_dn, cot, wfwd, *held)


def feature_part(half, kgs, gf, wbwd, taps):
    rows, _, width = kgs.shape
    channels = wbwd.shape[0] // 3
    vm = pl.BlockSpec(memory_space=pltpu.VMEM)
    rim_shape = (channels + 3 * (taps - 1), width)
    return pl.pallas_call(
        functools.partial(feature_kernel, taps),
        out_shape=[jax.ShapeDtypeStruct((channels * rows, width), F32),
                   jax.ShapeDtypeStruct((6, rows, width), F32),
                   jax.ShapeDtypeStruct(rim_shape, BF16), jax.ShapeDtypeStruct(rim_shape, BF16)],
        in_specs=[pl.BlockSpec(memory_space=pltpu.SMEM), vm, vm, vm],
        out_specs=[vm] * 4,
        scratch_shapes=[pltpu.VMEM((rows + 2, channels, width), F32), pltpu.VMEM(gf.shape[1:], F32),
                        pltpu.VMEM((2,) + rim_shape, BF16)],
        compiler_params=pltpu.CompilerParams(vmem_limit_bytes=VMEM_GRANT),
    )(half, kgs, gf, wbwd)


def halo_rows(feat, frames, taps):
    channels, rows, width = feat.shape
    shape = ((channels + 3 * (taps - 1), width), BF16)
    hbm, vm = pl.BlockSpec(memory_space=pltpu.HBM), pl.BlockSpec(memory_space=pltpu.VMEM)
    return pl.pallas_call(
        functools.partial(halo_kernel, taps),
        out_shape=[jax.ShapeDtypeStruct(*shape)] * 2,
        in_specs=[hbm, hbm],
        out_specs=[vm, vm],
        scratch_shapes=[pltpu.VMEM(feat.shape, BF16), pltpu.VMEM(frames.shape, BF16),
                        pltpu.VMEM((channels * rows, width), F32), pltpu.SemaphoreType.DMA((2,))],
    )(feat, frames)


def both_weights(hw, taps, channels):
    wfwd = order(hw, taps)
    wbwd = wfwd.reshape(128, 3, 3, channels).transpose(1, 3, 2, 0).reshape(3 * channels, 3 * 128)
    return wfwd, wbwd


def fan_kernel(parts_ref, out):
    total = jnp.sum(parts_ref[...], 0).astype(out.dtype)
    for n in range(out.shape[0]):
        out[n] = total


def fan(parts, count, dtype):
    return vmem_call(fan_kernel, [((count,) + parts.shape[1:], dtype)], [], parts)[0]


def unpack(parts, taps, columns, factor):
    return vmem_call(
        functools.partial(unpack_kernel, taps, factor), [((4 * taps, columns), F32)], [], parts)[0]


PLANE, LINE, TILE = ("y", "core", "x"), ("zl", "zh"), ("x", "zh")


def step(frames, features, cotangent, head_weight):
    taps = head_weight.shape[0] // 4
    rim = (taps - 1) // 2
    feat, frame, cot = features[0], frames[0], cotangent[0]
    channels, rows, width = feat.shape
    tiles, plane, line = lax.axis_size(TILE), lax.axis_size(PLANE), lax.axis_size(LINE)
    down = [(i, i + 1) for i in range(tiles - 1)]
    up = [(i + 1, i) for i in range(tiles - 1)]

    first, last = halo_rows(feat, frame, taps)
    halo_up = lax.ppermute(last, TILE, down)
    halo_dn = lax.ppermute(first, TILE, up)
    wfwd, wbwd = both_weights(head_weight, taps, channels)
    held = early(feat, frame, cot, wfwd, taps)
    parts, kgs, gf = late(halo_up, halo_dn, cot, wfwd, held, taps, plane)

    terms = lax.all_to_all(parts, PLANE, 0, 0)
    half = lax.axis_index("zh")
    gfeat, gframe, near, far = feature_part(half.reshape(1), kgs, gf, wbwd, taps)
    hopped = lax.ppermute(far, TILE, [(i, i - 2) for i in range(2, tiles, 2)]
                          + [(i, i + 2) for i in range(1, tiles - 2, 2)])
    rims = lax.ppermute(jnp.stack([near, hopped]), TILE, [(i, i ^ 1) for i in range(tiles)])
    near, far = rims[0], rims[1]
    terms = lax.all_to_all(fan(terms, line, F32), LINE, 0, 0)
    total = lax.all_to_all(fan(terms, plane, GATHER_TYPE), PLANE, 0, 0)
    from_up = jnp.where(half == 0, far, near).astype(F32)
    from_dn = jnp.where(half == 0, near, far).astype(F32)
    pixels = plane * line * rows * width
    grad_weight = unpack(total, taps, 9 * channels, pixels ** -0.5)

    gfeat = gfeat.reshape(channels, rows, width)
    gfeat = (gfeat + jnp.pad(from_up[:channels, None], ((0, 0), (0, rows - 1), (0, 0)))
             + jnp.pad(from_dn[:channels, None], ((0, 0), (rows - 1, 0), (0, 0))))
    gframe = (gframe
              + jnp.pad(from_up[channels:].reshape(6, rim, width), ((0, 0), (0, rows - rim), (0, 0)))
              + jnp.pad(from_dn[channels:].reshape(6, rim, width), ((0, 0), (rows - rim, 0), (0, 0))))
    return grad_weight, gfeat[None], gframe.reshape(1, 2, 3, rows, width)


def solution(mesh):
    fine = Mesh(mesh.devices.reshape(8, 4, 2, 4, 2), ("zl", "y", "core", "x", "zh"))
    pairs, tile = ("zl", "y", "core"), ("x", "zh")
    in_specs = (
        P(pairs, None, None, tile, None),
        P(pairs, None, tile, None),
        P(pairs, None, tile, None),
        P(),
    )
    out_specs = (P(), P(pairs, None, tile, None), P(pairs, None, None, tile, None))
    return jax.shard_map(step, mesh=fine, in_specs=in_specs, out_specs=out_specs, check_vma=False)
```

```python
import functools
import jax
import jax.numpy as jnp
from jax import lax
from jax.experimental import pallas as pl
from jax.experimental.pallas import tpu as pltpu
from jax.sharding import Mesh, PartitionSpec as P


F32, BF16 = jnp.float32, jnp.bfloat16
UNROLL_EARLY = 7
UNROLL_LATE = 7
UNROLL_FEATURE = 8
GATHER_TYPE = BF16
VMEM_GRANT = 16 * 1024 * 1024


def dims(a, b):
    return (((a,), (b,)), ((), ()))


def split(v):
    hi = v.astype(BF16)
    lo = (v - hi.astype(F32)).astype(BF16)
    return hi, lo


def column_bands(taps, width):
    rim = (taps - 1) // 2
    lane = lax.broadcasted_iota(jnp.int32, (width, width), 1)
    sub = lax.broadcasted_iota(jnp.int32, (width, width), 0)
    bands = []
    for f in range(2):
        tap = (lane - sub + (2 * width - 64 * f)) % width
        at = sub + tap - rim
        bands.append((tap < taps) & (at >= 0) & (at < width))
    return lane, sub, bands


def three_columns(row):
    lane = lax.broadcasted_iota(jnp.int32, row.shape, 1)
    width = row.shape[1]
    left = jnp.where(lane == 0, 0.0, pltpu.roll(row, 1, 1))
    right = jnp.where(lane == width - 1, 0.0, pltpu.roll(row, width - 1, 1))
    return jnp.concatenate([left, row, right], 0).astype(BF16)


def frame_terms(taps, k, g, bands):
    skew = pltpu.roll((k * taps ** -0.5).T, 0, 1, stride=1, stride_axis=0)
    out = []
    for f in range(2):
        v = k[64 * f + 32:64 * f + 64] * taps ** -0.5
        u_hi, u_lo = split(jnp.concatenate([v * g[c] for c in range(3)], 0))
        b_hi, b_lo = split(jnp.where(bands[f], skew, 0.0))
        w = jnp.dot(
            jnp.concatenate([u_hi, u_hi, u_lo], 1),
            jnp.concatenate([b_hi, b_lo, b_hi], 0), preferred_element_type=F32)
        out.append((jnp.concatenate([b_hi, b_lo], 1), jnp.concatenate([u_hi, u_lo], 0), w))
    return out


def early_kernel(taps, feat, frames, cot, wfwd, fb, bst, ust, gf, ip, fs):
    channels, rows, width = feat.shape
    rim = (taps - 1) // 2
    for n in range(6):
        ip[n] = jnp.zeros(ip.shape[1:], F32)
        ip[n, rim:rim + rows] = pltpu.roll(frames[n // 3, n % 3].astype(F32), rim + 64 * (n // 3), 1)
    fs[...] = feat[...].astype(F32).reshape(channels * rows, width)
    for y in range(rows):
        fb[y] = three_columns(fs[pl.ds(y, channels, stride=rows), :])
    gf[...] = jnp.zeros_like(gf)
    _, _, bands = column_bands(taps, width)

    def step(m, carry):
        ya = 2 * m + 1
        pair = jnp.concatenate(
            [fb[pl.ds(ya + h - 1, 3)].reshape(9 * channels, width) for h in range(2)], 1)
        k = jnp.dot(wfwd[...], pair, preferred_element_type=F32)
        for h in range(2):
            y = ya + h
            g = [cot[c, pl.ds(y, 1), :] for c in range(3)]
            terms = frame_terms(taps, k[:, width * h:width * (h + 1)], g, bands)
            for f, (b, u, w) in enumerate(terms):
                bst[y - 1, f] = b
                ust[y - 1, f] = u
                for c in range(3):
                    gf[3 * f + c, pl.ds(y, 32), :] += w[32 * c:32 * c + 32]
        return carry

    lax.fori_loop(0, rows // 2 - 1, step, 0, unroll=UNROLL_EARLY)


def late_kernel(taps, halo_up, halo_dn, cot, wfwd, fb, bst, ust, gf_in, ip_in,
                parts_ref, kgs, gf, ip, wg):
    rim = (taps - 1) // 2
    rows, channels, width = fb.shape[0], fb.shape[1] // 3, fb.shape[2]
    _, sub, bands = column_bands(taps, width)
    head = three_columns(halo_up[:channels].astype(F32))
    foot = three_columns(halo_dn[:channels].astype(F32))
    edges = jnp.concatenate([
        jnp.concatenate([head, fb[0], fb[1]], 0),
        jnp.concatenate([fb[rows - 2], fb[rows - 1], foot], 0)], 1)
    k = jnp.dot(wfwd[...], edges, preferred_element_type=F32)

    ip[...] = ip_in[...]
    for n in range(6):
        at = channels + n * rim
        turn = rim + 64 * (n // 3)
        ip[n, :rim] = pltpu.roll(halo_up[at:at + rim].astype(F32), turn, 1)
        ip[n, rim + rows:rim + rows + rim] = pltpu.roll(halo_dn[at:at + rim].astype(F32), turn, 1)
    gf[...] = gf_in[...]

    def tap_grads(y, terms):
        g = [cot[c, pl.ds(y, 1), :] for c in range(3)]
        grads = []
        horiz = None
        for f, (b, u) in enumerate(terms):
            window = jnp.concatenate(
                [ip[3 * f + c, pl.ds(y, 32), :] for c in range(3)], 0).astype(BF16)
            blended = lax.dot_general(
                jnp.concatenate([window, window], 1), b, dims(1, 1), preferred_element_type=F32)
            grads.append(sum(g[c] * blended[32 * c:32 * c + 32] for c in range(3)))
            d = lax.dot_general(
                u, jnp.concatenate([window, window], 0), dims(0, 0), preferred_element_type=F32)
            horiz = jnp.where(bands[f], d, 0.0 if f == 0 else horiz)
        turned = [horiz[:8]]
        for r in range(1, width // 8):
            turned.append(pltpu.roll(horiz[8 * r:8 * r + 8], width - 8 * r, 1))
        horiz = jnp.concatenate(turned, 0)
        for bit in range(3):
            horiz = jnp.where((sub & (1 << bit)) != 0, pltpu.roll(horiz, width - (1 << bit), 1), horiz)
        ht = horiz.T
        kg = jnp.concatenate([ht[:32], grads[0], ht[64:96], grads[1]], 0) * taps ** -0.5
        kg = kg.astype(BF16)
        kgs[y] = kg
        return kg

    pair_kg = []
    for h, y in enumerate((0, rows - 1)):
        g = [cot[c, y:y + 1, :] for c in range(3)]
        terms = frame_terms(taps, k[:, width * h:width * (h + 1)], g, bands)
        for f, (_, _, w) in enumerate(terms):
            for c in range(3):
                gf[3 * f + c, y:y + 32] += w[32 * c:32 * c + 32]
        pair_kg.append(tap_grads(y, [t[:2] for t in terms]))
    wg[...] = lax.dot_general(
        jnp.concatenate(pair_kg, 1), edges, dims(1, 1), preferred_element_type=F32)

    def step(m, carry):
        ya = 2 * m + 1
        pair = jnp.concatenate(
            [fb[pl.ds(ya + h - 1, 3)].reshape(9 * channels, width) for h in range(2)], 1)
        pair_kg = [
            tap_grads(ya + h, [(bst[ya + h - 1, f], ust[ya + h - 1, f]) for f in range(2)])
            for h in range(2)]
        wg[...] += lax.dot_general(
            jnp.concatenate(pair_kg, 1), pair, dims(1, 1), preferred_element_type=F32)
        return carry

    lax.fori_loop(0, rows // 2 - 1, step, 0, unroll=UNROLL_LATE)
    pack(wg, parts_ref, taps)


def feature_kernel(taps, half, kgs, gf, wbwd, gfeat, gframe, rims, acc, turned):
    rim = (taps - 1) // 2
    rows, _, width = kgs.shape
    channels = acc.shape[1]
    lane = lax.broadcasted_iota(jnp.int32, (128, width), 1)
    acc[...] = jnp.zeros_like(acc)

    def step(m, carry):
        wide = []
        for h in range(2):
            kg = kgs[2 * m + h].astype(F32)
            wide.append(jnp.concatenate([
                jnp.where(lane == width - 1, 0.0, pltpu.roll(kg, width - 1, 1)),
                kg,
                jnp.where(lane == 0, 0.0, pltpu.roll(kg, 1, 1))], 0).astype(BF16))
        part = jnp.dot(wbwd[...], jnp.concatenate(wide, 1), preferred_element_type=F32)
        for h in range(2):
            for a in range(3):
                acc[2 * m + h + a] += part[channels * a:channels * (a + 1), width * h:width * (h + 1)]
        return carry

    lax.fori_loop(0, rows // 2, step, 0, unroll=UNROLL_FEATURE)

    for y in range(rows):
        gfeat[pl.ds(y, channels, stride=rows), :] = acc[y + 1]
    up, dn = 1 - half[0], half[0]
    rims[up, :channels] = acc[0].astype(BF16)
    rims[dn, :channels] = acc[rows + 1].astype(BF16)
    for n in range(6):
        turned[...] = pltpu.roll(gf[n], width - rim - 64 * (n // 3), 1)
        gframe[n] = turned[rim:rim + rows]
        at = channels + n * rim
        rims[up, at:at + rim] = turned[:rim].astype(BF16)
        rims[dn, at:at + rim] = turned[rim + rows:rim + rows + rim].astype(BF16)


def pack(wg, parts, taps):
    count, size, _ = parts.shape
    full, high = wg.shape[1] // 128, 4 * taps
    value = jnp.concatenate([wg[32 * g:32 * g + taps] for g in (1, 0, 3, 2)], 0)
    tail = value[:, 128 * full:]
    flat = jnp.concatenate(
        [value[:, 128 * n:128 * (n + 1)] for n in range(full)]
        + [jnp.concatenate([tail[:high // 2], tail[high // 2:]], 1)], 0)
    flat = jnp.concatenate([flat, jnp.zeros((count * size - flat.shape[0], 128), F32)], 0)
    parts[...] = flat.reshape(count, size, 128)


def unpack_kernel(taps, factor, parts, out):
    count, size, _ = parts.shape
    full, high = out.shape[1] // 128, 4 * taps
    flat = parts[...].astype(F32).reshape(count * size, 128) * factor
    for n in range(full):
        out[:, 128 * n:128 * (n + 1)] = flat[high * n:high * (n + 1)]
    tail = flat[high * full:high * full + high // 2]
    out[:, 128 * full:] = jnp.concatenate([tail[:, :64], tail[:, 64:]], 0)


def halo_kernel(taps, feat_hbm, frames_hbm, cot_hbm, first, last, feat, frames, cot, fs, sems):
    rim = (taps - 1) // 2
    copies = [pltpu.make_async_copy(feat_hbm, feat, sems.at[0]),
              pltpu.make_async_copy(frames_hbm, frames, sems.at[1]),
              pltpu.make_async_copy(cot_hbm, cot, sems.at[2])]
    for copy in copies:
        copy.start()
    for copy in copies:
        copy.wait()
    channels, rows, width = feat.shape
    fs[...] = feat[...].astype(F32).reshape(channels * rows, width)
    first[:channels] = fs[pl.ds(0, channels, stride=rows), :].astype(BF16)
    last[:channels] = fs[pl.ds(rows - 1, channels, stride=rows), :].astype(BF16)
    for n in range(6):
        frame = frames[n // 3, n % 3].astype(F32)
        at = channels + n * rim
        first[at:at + rim] = frame[:rim].astype(BF16)
        last[at:at + rim] = frame[rows - rim:].astype(BF16)


def finish_kernel(taps, half, gfeat, gframe, near, far, out_feat, out_frame, rims):
    rim = (taps - 1) // 2
    channels = near.shape[0] - 6 * rim
    rows = gframe.shape[1]
    rims[0] = near[...].astype(F32)
    rims[1] = far[...].astype(F32)
    up, dn = 1 - half[0], half[0]
    out_feat[...] = gfeat[...]
    out_feat[pl.ds(0, channels, stride=rows), :] += rims[up, :channels]
    out_feat[pl.ds(rows - 1, channels, stride=rows), :] += rims[dn, :channels]
    out_frame[...] = gframe[...]
    for n in range(6):
        at = channels + n * rim
        out_frame[n, :rim] += rims[up, at:at + rim]
        out_frame[n, rows - rim:] += rims[dn, at:at + rim]


def order(hw, taps):
    hw = hw.reshape(2, 2, taps, -1)[:, ::-1]
    return jnp.pad(hw, ((0, 0), (0, 0), (0, 32 - taps), (0, 0))).reshape(128, -1)


def vmem_call(kernel, outs, scratch, *operands):
    vm = pl.BlockSpec(memory_space=pltpu.VMEM)
    return pl.pallas_call(
        kernel,
        out_shape=[jax.ShapeDtypeStruct(*o) for o in outs],
        in_specs=[vm] * len(operands),
        out_specs=[vm] * len(outs),
        scratch_shapes=[pltpu.VMEM(*o) for o in scratch],
        compiler_params=pltpu.CompilerParams(vmem_limit_bytes=VMEM_GRANT),
    )(*operands)


def early(feat, frames, cot, wfwd, taps):
    channels, rows, width = feat.shape
    return vmem_call(
        functools.partial(early_kernel, taps),
        [((rows, 3 * channels, width), BF16), ((rows - 2, 2, width, 2 * width), BF16),
         ((rows - 2, 2, 192, width), BF16), ((6, rows + 32, width), F32), ((6, rows + 32, width), F32)],
        [((channels * rows, width), F32)],
        feat, frames, cot, wfwd)


def late(halo_up, halo_dn, cot, wfwd, held, taps, parts):
    rows, width = held[0].shape[0], held[0].shape[2]
    columns = 3 * held[0].shape[1]
    size = -(-4 * taps * columns // (128 * parts * 8)) * 8
    return vmem_call(
        functools.partial(late_kernel, taps),
        [((parts, size, 128), F32), ((rows, 128, width), BF16), ((6, rows + 32, width), F32)],
        [((6, rows + 32, width), F32), ((128, columns), F32)],
        halo_up, halo_dn, cot, wfwd, *held)


def feature_part(half, kgs, gf, wbwd, taps):
    rows, _, width = kgs.shape
    channels = wbwd.shape[0] // 3
    vm = pl.BlockSpec(memory_space=pltpu.VMEM)
    return pl.pallas_call(
        functools.partial(feature_kernel, taps),
        out_shape=[jax.ShapeDtypeStruct((channels * rows, width), F32),
                   jax.ShapeDtypeStruct((6, rows, width), F32),
                   jax.ShapeDtypeStruct((2, channels + 3 * (taps - 1), width), BF16)],
        in_specs=[pl.BlockSpec(memory_space=pltpu.SMEM), vm, vm, vm],
        out_specs=[vm] * 3,
        scratch_shapes=[pltpu.VMEM((rows + 2, channels, width), F32), pltpu.VMEM(gf.shape[1:], F32)],
        compiler_params=pltpu.CompilerParams(vmem_limit_bytes=VMEM_GRANT),
    )(half, kgs, gf, wbwd)


def halo_rows(feat, frames, cot, taps):
    channels, rows, width = feat.shape
    shape = (channels + 3 * (taps - 1), width)
    hbm, vm = pl.BlockSpec(memory_space=pltpu.HBM), pl.BlockSpec(memory_space=pltpu.VMEM)
    held = [pltpu.with_memory_space_constraint(v, pltpu.HBM) for v in (feat, frames, cot)]
    return pl.pallas_call(
        functools.partial(halo_kernel, taps),
        out_shape=[jax.ShapeDtypeStruct(shape, BF16)] * 2
        + [jax.ShapeDtypeStruct(v.shape, v.dtype) for v in (feat, frames, cot)],
        in_specs=[hbm] * 3,
        out_specs=[vm] * 5,
        scratch_shapes=[pltpu.VMEM((channels * rows, width), F32), pltpu.SemaphoreType.DMA((3,))],
        compiler_params=pltpu.CompilerParams(vmem_limit_bytes=VMEM_GRANT),
    )(*held)


def finish(half, gfeat, gframe, near, far, taps):
    vm = pl.BlockSpec(memory_space=pltpu.VMEM)
    return pl.pallas_call(
        functools.partial(finish_kernel, taps),
        out_shape=[jax.ShapeDtypeStruct(v.shape, F32) for v in (gfeat, gframe)],
        in_specs=[pl.BlockSpec(memory_space=pltpu.SMEM)] + [vm] * 4,
        out_specs=[vm] * 2,
        scratch_shapes=[pltpu.VMEM((2,) + near.shape, F32)],
        compiler_params=pltpu.CompilerParams(vmem_limit_bytes=VMEM_GRANT),
    )(half, gfeat, gframe, near, far)


def both_weights(hw, taps, channels):
    wfwd = order(hw, taps)
    wbwd = wfwd.reshape(128, 3, 3, channels).transpose(1, 3, 2, 0).reshape(3 * channels, 3 * 128)
    return wfwd, wbwd


def fan_kernel(parts_ref, out):
    total = jnp.sum(parts_ref[...], 0).astype(out.dtype)
    for n in range(out.shape[0]):
        out[n] = total


def fan(parts, count, dtype):
    return vmem_call(fan_kernel, [((count,) + parts.shape[1:], dtype)], [], parts)[0]


def unpack(parts, taps, columns, factor):
    return vmem_call(
        functools.partial(unpack_kernel, taps, factor), [((4 * taps, columns), F32)], [], parts)[0]


PLANE, LINE, TILE = ("y", "core", "x"), ("zl", "zh"), ("x", "zh")


def step(frames, features, cotangent, head_weight):
    taps = head_weight.shape[0] // 4
    feat, frame, cot = features[0], frames[0], cotangent[0]
    channels, rows, width = feat.shape
    tiles, plane, line = lax.axis_size(TILE), lax.axis_size(PLANE), lax.axis_size(LINE)
    down = [(i, i + 1) for i in range(tiles - 1)]
    up = [(i + 1, i) for i in range(tiles - 1)]

    first, last, feat, frame, cot = halo_rows(feat, frame, cot, taps)
    halo_up = lax.ppermute(last, TILE, down)
    halo_dn = lax.ppermute(first, TILE, up)
    wfwd, wbwd = both_weights(head_weight, taps, channels)
    held = early(feat, frame, cot, wfwd, taps)
    parts, kgs, gf = late(halo_up, halo_dn, cot, wfwd, held, taps, plane)

    terms = lax.all_to_all(parts, PLANE, 0, 0)
    half = lax.axis_index("zh")
    gfeat, gframe, rims = feature_part(half.reshape(1), kgs, gf, wbwd, taps)
    rims = lax.ppermute(rims, TILE, [(i, i ^ 1) for i in range(tiles)])
    near = rims[0]
    far = lax.ppermute(rims[1], TILE, [(i, i + 2) for i in range(0, tiles - 2, 2)]
                       + [(i, i - 2) for i in range(3, tiles, 2)])
    terms = lax.all_to_all(fan(terms, line, F32), LINE, 0, 0)
    total = lax.all_to_all(fan(terms, plane, GATHER_TYPE), PLANE, 0, 0)
    pixels = plane * line * rows * width
    grad_weight = unpack(total, taps, 9 * channels, pixels ** -0.5)
    gfeat, gframe = finish(half.reshape(1), gfeat, gframe, near, far, taps)
    return (grad_weight, gfeat.reshape(1, channels, rows, width),
            gframe.reshape(1, 2, 3, rows, width))


def solution(mesh):
    fine = Mesh(mesh.devices.reshape(8, 4, 2, 4, 2), ("zl", "y", "core", "x", "zh"))
    pairs, tile = ("zl", "y", "core"), ("x", "zh")
    in_specs = (
        P(pairs, None, None, tile, None),
        P(pairs, None, tile, None),
        P(pairs, None, tile, None),
        P(),
    )
    out_specs = (P(), P(pairs, None, tile, None), P(pairs, None, None, tile, None))
    return jax.shard_map(step, mesh=fine, in_specs=in_specs, out_specs=out_specs, check_vma=False)
```
